256 devices in a mesh: freq: 64 (over x, z_lo, y), chan: 4 (over z_hi, core).
Axes of the slice: x: 4, y: 4, z: 8 (z_hi: 2, z_lo: 4; z = z_hi * 4 + z_lo), core: 2. Of those that a mesh axis runs over, the one named last changes fastest.
Arguments:
- factor: bfloat16 [512, 2, 128, 128], P('freq', None, 'chan'), may hold values from -0.2 to 1.2, as said below
- spectrum: bfloat16 [512, 2, 128, 128], P('freq', None, 'chan'), may hold values from -2 to 5, as said below
- guess_scale: float32 [512], P('freq'), may hold values from 0.1 to 0.3
- lag_cutoff: int32 [1], replicated, may hold values from 64 to 255
Outputs:
- new_factor: float32 [512, 2, 128, 128], P('freq', None, None, 'chan')
The draws below stay inside these ranges and needn't reach their ends.
Inputs may be any that keep to these rules, and one draw needn't show every extreme that they name: The real part of factor is the identity plus independent entries of spread about 0.35 / sqrt(128). At every frequency spectrum is Hermitian: its real part symmetric, its imaginary part antisymmetric with a zero diagonal; it is positive definite.
All inputs are finite; a program needn't handle non-finite values.
Results may differ from the reference program's by a relative error of at most 0.00105.
Values may be sent and summed in bfloat16 or wider, within the bound.
A program may use at most 64 MiB of HBM per device.

```python
import math
import jax
import jax.numpy as jnp
from jax import lax

C = 128
F = 512
ITERS = 8


def noise_pair(key, shape):
    key_a = jax.random.fold_in(key, 17)
    key_b = jax.random.fold_in(key, 29)
    first_noise = jnp.clip(jax.random.normal(key_a, shape, jnp.float32), -4.0, 4.0)
    second_noise = jnp.clip(jax.random.normal(key_b, shape, jnp.float32), -4.0, 4.0)
    return (first_noise, second_noise)


def draw_factor(key, part):
    first_noise, second_noise = noise_pair(key, (F, C, C))
    spread = 0.35 / math.sqrt(C)
    part_re = jnp.eye(C, dtype=jnp.float32)[None] + spread * first_noise
    part_im = spread * second_noise
    return jnp.stack([part_re, part_im], axis=1).astype(jnp.bfloat16)


def draw_spectrum(key, part):
    first_noise, second_noise = noise_pair(key, (F, C, C))
    spread = 0.25 / math.sqrt(C)
    part_re = spread * (first_noise + jnp.swapaxes(first_noise, 1, 2)) + 1.5 * jnp.eye(C, dtype=jnp.float32)[None]
    part_im = spread * (second_noise - jnp.swapaxes(second_noise, 1, 2))
    logs = jax.random.uniform(jax.random.fold_in(key, 41), (F, C), jnp.float32, math.log(0.5), math.log(2.0))
    roots = jnp.exp(0.5 * logs)
    outer_scale = roots[:, :, None] * roots[:, None, :]
    return jnp.stack([part_re * outer_scale, part_im * outer_scale], axis=1).astype(jnp.bfloat16)


def levels(own_key, shape, cuts, low, high):
    def one(position, shards_of):
        steps = jax.random.uniform(jax.random.fold_in(jax.random.fold_in(own_key, 6), position), (shards_of,), jnp.float32, low / len(cuts), high / len(cuts))
        return jnp.repeat(jnp.exp(steps), shape[position] // shards_of).reshape((-1,) + (1,) * (len(shape) - position - 1))

    level = one(*cuts[0])
    for cut in cuts[1:]:
        level = level * one(*cut)
    return level


def setup_inputs(seed: int = 0) -> dict:
    key_of = jax.random.split(jax.random.key(seed), 5)
    return {
        "factor": draw_factor(jax.random.fold_in(key_of[4], 71), 0),
        "spectrum": draw_spectrum(jax.random.fold_in(key_of[4], 71), 0),
        "guess_scale": jnp.clip(jnp.exp(math.log(0.3) - 1.0986123 * jax.random.uniform(key_of[2], (F,), jnp.float32) ** levels(key_of[2], (F,), ((0, 64),), -0.2, 0.2)), 0.1, 0.3),
        "lag_cutoff": jax.random.randint(key_of[3], (1,), F // 8, F // 2).astype(jnp.int32),
    }


def matmul(matrix_a, matrix_b):
    return jnp.einsum("fij,fjk->fik", matrix_a, matrix_b, precision=lax.Precision.HIGHEST)


def complex_product(left, right):
    left_re, left_im = left[:, 0], left[:, 1]
    right_re, right_im = right[:, 0], right[:, 1]
    part_re = matmul(left_re, right_re) - matmul(left_im, right_im)
    part_im = matmul(left_re, right_im) + matmul(left_im, right_re)
    return jnp.stack([part_re, part_im], axis=1)


def adjoint(matrix):
    return jnp.stack([jnp.swapaxes(matrix[:, 0], -1, -2), -jnp.swapaxes(matrix[:, 1], -1, -2)], axis=1)


def reference(factor, spectrum, guess_scale, lag_cutoff):
    factor_f = factor.astype(jnp.float32)
    spectrum_f = spectrum.astype(jnp.float32)
    inverse = guess_scale.astype(jnp.float32)[:, None, None, None] * adjoint(factor_f)
    for iteration in range(ITERS):
        inverse = 2.0 * inverse - complex_product(complex_product(inverse, factor_f), inverse)
    middle = complex_product(complex_product(inverse, spectrum_f), adjoint(inverse))
    middle = middle.at[:, 0].add(jnp.eye(C, dtype=jnp.float32))
    complex_g = lax.complex(middle[:, 0], middle[:, 1])
    lag_terms = jnp.fft.ifft(complex_g, axis=0)
    lag_index = jnp.arange(F, dtype=jnp.int32)
    keep = jnp.where(lag_index == 0, 0.5, jnp.where((lag_index >= 1) & (lag_index <= lag_cutoff[0]), 1.0, 0.0))
    projected = jnp.fft.fft(lag_terms * keep[:, None, None], axis=0)
    causal = jnp.stack([jnp.real(projected), jnp.imag(projected)], axis=1).astype(jnp.float32)
    return complex_product(factor_f, causal)
```

```python
import functools

import jax
import jax.numpy as jnp
import numpy as np
from jax import lax
from jax.experimental import pallas as pl
from jax.experimental.pallas import tpu as pltpu
from jax.sharding import PartitionSpec as P

ITERS = 8
MESH = pl.DeviceIdType.MESH
BF = jnp.bfloat16
F32 = jnp.float32
C = 128
PANEL = 32
FL = 8
OWN = 2
G = 64
F = 512
LAGS = 256
Z_ORDER = (4, 3, 5, 2, 6, 1, 7, 0)
XY_ORDER = (2, 1, 3, 0)


def rem(a, b):
    return lax.rem(a, jnp.int32(b))


def div(a, b):
    return lax.div(a, jnp.int32(b))


def coords():
    f = lax.axis_index("freq")
    c = lax.axis_index("chan")
    return div(f, 16), rem(f, 4), div(c, 2) * 4 + rem(div(f, 4), 4), rem(c, 2)


def place(x, y, z, k):
    return (x * 4 + rem(z, 4)) * 4 + y, div(z, 4) * 2 + k


def split(value):
    high = value.astype(BF)
    return high, (value - high.astype(F32)).astype(BF)


def embed(value):
    re, im = value[:, :C], value[:, C:]
    return jnp.concatenate([value, jnp.concatenate([-im, re], axis=1)], axis=0)


def dot(left, right):
    return jnp.dot(left, right, preferred_element_type=F32)


def dot_nt(left, right):
    return lax.dot_general(left, right, (((1,), (1,)), ((), ())), preferred_element_type=F32)


def dot_tn(left, right):
    return lax.dot_general(left, right, (((0,), (0,)), ((), ())), preferred_element_type=F32)


def dot_tt(left, right):
    return lax.dot_general(left, right, (((0,), (1,)), ((), ())), preferred_element_type=F32)


def tables():
    lag = np.arange(LAGS)[:, None]
    freq = np.arange(F)[None, :]
    angle = 2.0 * np.pi * ((lag * freq) % F) / F
    cos, sin = np.cos(angle), np.sin(angle)
    to_lag = np.concatenate([cos, sin], axis=1) / F
    to_freq = np.concatenate([cos.T, -sin.T], axis=1)

    def halves(table):
        high = table.astype(jnp.bfloat16)
        low = (table - high.astype(np.float64)).astype(jnp.bfloat16)
        return np.concatenate([high, low], axis=0)

    return halves(to_lag), halves(to_freq)


def turn(value, lane):
    ahead = pltpu.roll(value, 96, 1)
    behind = pltpu.roll(value, 32, 1)
    return jnp.where(rem(lane, 64) < 32, -ahead, behind)


def table_apply(table_ref, rows, value, lane):
    high, low = split(value)
    turn_high, turn_low = turn(value, lane), None
    turn_high, turn_low = split(turn_high)
    both = jnp.concatenate(
        [jnp.concatenate([high, low], axis=1), jnp.concatenate([turn_high, turn_low], axis=1)], axis=0
    )
    first = dot(table_ref[0:rows, :], both)
    second = dot(table_ref[rows : 2 * rows, :], jnp.concatenate([high, turn_high], axis=0))
    return first[:, :C] + first[:, C:] + second


def kernel(
    factor_ref, spectrum_ref, psi_ref, scale_ref, cutoff_ref, to_lag_hbm, to_freq_hbm, out_ref,
    spec_all, psi_all, send_f, recv_f, send_r, recv_r, to_lag, to_freq,
    stage_sem, table_sem, local_sem, spec_ss, spec_rs, psi_ss, psi_rs, relay_ss, relay_rs, fwd_ss, fwd_rs, fwd_ls, ret_ss, ret_rs, ret_ls,
):
    x, y, z, k = coords()
    me_f = lax.axis_index("freq")
    me_c = lax.axis_index("chan")
    me_lin = me_f * 4 + me_c

    on_x = [place(rem(x + i, 4), y, z, k) for i in (1, 2, 3)]
    on_y = [place(x, rem(y + i, 4), z, k) for i in (1, 2, 3)]
    on_z = [place(x, y, rem(z + i, 8), k) for i in range(1, 8)]
    sibling = place(x, y, z, 1 - k)
    across = place(x, y, rem(z + 4, 8), k)
    diagonal = place(x, y, rem(z + 4, 8), 1 - k)

    def signal(sem, peers):
        for peer in peers:
            pl.semaphore_signal(sem, inc=1, device_id=peer, device_id_type=MESH)

    barrier = pltpu.get_barrier_semaphore()
    first_peers = on_x + on_y + on_z + [sibling, diagonal]
    signal(barrier, first_peers)

    tables_in = [
        pltpu.make_async_copy(to_lag_hbm, to_lag, table_sem.at[0]),
        pltpu.make_async_copy(to_freq_hbm, to_freq, table_sem.at[1]),
    ]
    for copy in tables_in:
        copy.start()

    my_rows = pl.ds(pl.multiple_of(me_c * PANEL, PANEL), PANEL)
    own_copies = [
        pltpu.make_async_copy(factor_ref, psi_all.at[:, :, my_rows, :], local_sem.at[0]),
        pltpu.make_async_copy(spectrum_ref.at[pl.ds(OWN * me_c, OWN)], spec_all.at[:, :, my_rows, :], local_sem.at[1]),
    ]
    for copy in own_copies:
        copy.start()

    def remote(src, dst, send_sem, recv_sem, peer):
        return pltpu.make_async_remote_copy(
            src_ref=src, dst_ref=dst, send_sem=send_sem, recv_sem=recv_sem, device_id=peer, device_id_type=MESH
        )

    row = lax.broadcasted_iota(jnp.int32, (C, 2 * C), 0)
    col = lax.broadcasted_iota(jnp.int32, (C, 2 * C), 1)
    eye = (row == col).astype(F32)
    lane = lax.broadcasted_iota(jnp.int32, (G, C), 1)

    psis, rs, qs = [], [], []
    for b in range(OWN):
        psi = jnp.concatenate([psi_ref[b, 0], psi_ref[b, 1]], axis=1)
        wide = embed(psi)
        r = eye - scale_ref[OWN * me_c + b] * dot_nt(psi, jnp.concatenate([psi, jnp.concatenate([-psi[:, C:], psi[:, :C]], axis=1)], axis=0))
        psis.append(wide)
        rs.append(r)
        qs.append(eye + r)

    copies = []
    for step in range(1, ITERS):
        for b in range(OWN):
            r_high, r_low = split(rs[b])
            q_high, q_low = split(qs[b])
            square_left = jnp.concatenate([r_high, r_low, r_high], axis=1)
            e_high, e_low = embed(r_high), embed(r_low)
            right = jnp.concatenate([e_high, e_high, e_low], axis=0)
            r_next = dot(square_left, right)
            rs[b] = r_next
            n_high, n_low = split(r_next)
            en_high, en_low = embed(n_high), embed(n_low)
            qs[b] = qs[b] + dot(
                jnp.concatenate([q_high, q_low, q_high], axis=1), jnp.concatenate([en_high, en_high, en_low], axis=0)
            )
        if step == 1:
            pl.semaphore_wait(barrier, len(first_peers))
            for peer in (across, diagonal, sibling):
                copies.append(
                    remote(
                        spectrum_ref.at[pl.ds(OWN * peer[1], OWN)], spec_all.at[:, :, my_rows, :], spec_ss, spec_rs, peer
                    )
                )
                copies[-1].start()
            for peer in (across, sibling):
                i = 0 if peer is across else 1
                remote(factor_ref, psi_all.at[:, :, my_rows, :], psi_ss.at[i], psi_rs.at[i], peer).start()
            signal(stage_sem.at[0], [sibling])
        if step == 3:
            pl.semaphore_wait(stage_sem.at[0], 1)
            signal(stage_sem.at[1], on_y)
        if step == 5:
            pl.semaphore_wait(stage_sem.at[1], 3)
            signal(stage_sem.at[2], on_z)

    own_copies[1].wait()
    three = spec_all.at[:, :, pl.ds(0, 3 * PANEL), :]
    pltpu.make_async_copy(three, three, spec_rs).wait()

    for b in range(OWN):
        q_high, q_low = split(qs[b])
        zz = scale_ref[OWN * me_c + b] * dot(
            jnp.concatenate([q_high, q_low], axis=1), jnp.concatenate([psis[b], psis[b]], axis=0)
        )
        z_high, z_low = split(zz)
        spec = jnp.concatenate([spec_all[b, 0], spec_all[b, 1]], axis=1)
        u = dot(
            jnp.concatenate([spec, spec], axis=1), jnp.concatenate([embed(z_high), embed(z_low)], axis=0)
        )
        u_high, u_low = split(u)

        def upright(value):
            return jnp.concatenate([value[:, :C], -value[:, C:]], axis=0)

        zs_high, zs_low = upright(z_high), upright(z_low)
        eu_high, eu_low = embed(u_high), embed(u_low)
        mid = eye + dot_tn(
            jnp.concatenate([zs_high, zs_low, zs_high], axis=0), jnp.concatenate([eu_high, eu_high, eu_low], axis=0)
        )
        pieces = [mid[:G, :C], mid[:G, C:], mid[G:, :C], mid[G:, C:]]
        for j in range(4):
            rolled = []
            for i, piece in enumerate(pieces):
                shift = (32 * i - 32 * j) % C
                rolled.append(pltpu.roll(piece, shift, 1) if shift else piece)
            packed = jnp.where(
                lane < 64,
                jnp.where(lane < 32, rolled[0], rolled[1]),
                jnp.where(lane < 96, rolled[2], rolled[3]),
            )
            send_f[pl.ds(G * j, G), b, :] = packed

    pl.semaphore_wait(stage_sem.at[2], 7)
    mine = pltpu.make_async_copy(send_f.at[me_c * G + me_f], recv_f.at[me_lin], fwd_ls)
    mine.start()
    for dx in XY_ORDER:
        for dy in XY_ORDER:
            for dk in (1, 0):
                for dz in Z_ORDER:
                    if (dx, dy, dz, dk) == (0, 0, 0, 0):
                        continue
                    peer = place(rem(x + dx, 4), rem(y + dy, 4), rem(z + dz, 8), 1 - k if dk else k)
                    remote(send_f.at[peer[1] * G + peer[0]], recv_f.at[me_lin], fwd_ss, fwd_rs, peer).start()

    own_copies[0].wait()
    across_rows = pl.ds(pl.multiple_of(across[1] * PANEL, PANEL), PANEL)
    diagonal_rows = pl.ds(pl.multiple_of(diagonal[1] * PANEL, PANEL), PANEL)
    sibling_rows = pl.ds(pl.multiple_of(sibling[1] * PANEL, PANEL), PANEL)
    panel = psi_all.at[:, :, across_rows, :]
    pltpu.make_async_copy(panel, panel, psi_rs.at[0]).wait()
    relay = remote(panel, panel, relay_ss, relay_rs, sibling)
    relay.start()

    for copy in tables_in:
        copy.wait()
    most = recv_f.at[pl.ds(0, 4 * G - 1)]
    mine.wait()
    pltpu.make_async_copy(most, most, fwd_rs).wait()

    gathered = recv_f[...].reshape(F, C)
    lane_f = lax.broadcasted_iota(jnp.int32, (F, C), 1)
    lane_l = lax.broadcasted_iota(jnp.int32, (LAGS, C), 1)
    lag_row = lax.broadcasted_iota(jnp.int32, (LAGS, C), 0)
    keep = jnp.where(lag_row == 0, 0.5, jnp.where(lag_row <= cutoff_ref[0], 1.0, 0.0)).astype(F32)
    lags = table_apply(to_lag, LAGS, gathered, lane_f) * keep
    send_r[...] = table_apply(to_freq, F, lags, lane_l)

    me_eight = pl.ds(pl.multiple_of(me_f * FL, FL), FL)
    back = pltpu.make_async_copy(send_r.at[me_eight, :], recv_r.at[me_eight, :], ret_ls)
    back.start()
    for dx in XY_ORDER:
        for dy in XY_ORDER:
            for dz in (3, 1, 2, 0):
                if (dx, dy, dz) == (0, 0, 0):
                    continue
                other = (rem(x + dx, 4) * 4 + rem(rem(z, 4) + dz, 4)) * 4 + rem(y + dy, 4)
                eight = pl.ds(pl.multiple_of(other * FL, FL), FL)
                remote(send_r.at[eight, :], recv_r.at[me_eight, :], ret_ss, ret_rs, (other, me_c)).start()

    panel = psi_all.at[:, :, sibling_rows, :]
    pltpu.make_async_copy(panel, panel, psi_rs.at[1]).wait()
    panel = psi_all.at[:, :, diagonal_rows, :]
    pltpu.make_async_copy(panel, panel, relay_rs).wait()
    back.wait()
    most = recv_r.at[pl.ds(0, F - FL), :]
    pltpu.make_async_copy(most, most, ret_rs).wait()

    for f in range(FL):
        d = recv_r[pl.ds(f, G, stride=FL), :]
        high, low = split(d)
        stack = jnp.concatenate(
            [
                jnp.concatenate([high[:, :64], low[:, :64]], axis=1),
                jnp.concatenate([high[:, 64:], low[:, 64:]], axis=1),
            ],
            axis=0,
        )
        both = jnp.concatenate([psi_all[f, 0], psi_all[f, 1]], axis=0)
        got = dot_tt(stack, both)
        got = got[:64] + got[64:]
        out_ref[f, 0] = got[:32, :C] - got[32:, C:]
        out_ref[f, 1] = got[32:, :C] + got[:32, C:]

    for i in range(2):
        pltpu.make_async_copy(factor_ref, factor_ref, psi_ss.at[i]).wait()
    pltpu.make_async_copy(three, three, spec_ss).wait()
    relay.wait_send()
    most = send_f.at[pl.ds(0, 4 * G - 1)]
    pltpu.make_async_copy(most, most, fwd_ss).wait()
    most = send_r.at[pl.ds(0, F - FL), :]
    pltpu.make_async_copy(most, most, ret_ss).wait()


def step(factor, spectrum, guess_scale, lag_cutoff):
    to_lag, to_freq = tables()
    psi = lax.all_to_all(factor, "chan", split_axis=0, concat_axis=2, tiled=True)
    vmem = pl.BlockSpec(memory_space=pltpu.VMEM)
    smem = pl.BlockSpec(memory_space=pltpu.SMEM)
    hbm = pl.BlockSpec(memory_space=pl.ANY)
    dma = pltpu.SemaphoreType.DMA
    out = pl.pallas_call(
        kernel,
        out_shape=jax.ShapeDtypeStruct((FL, 2, PANEL, C), F32),
        in_specs=[vmem, vmem, vmem, smem, smem, hbm, hbm],
        out_specs=vmem,
        scratch_shapes=[
            pltpu.VMEM((OWN, 2, C, C), BF),
            pltpu.VMEM((FL, 2, C, C), BF),
            pltpu.VMEM((4 * G, OWN, C), F32),
            pltpu.VMEM((4 * G, OWN, C), F32),
            pltpu.VMEM((F, C), F32),
            pltpu.VMEM((F, C), F32),
            pltpu.VMEM(to_lag.shape, BF),
            pltpu.VMEM(to_freq.shape, BF),
            pltpu.SemaphoreType.REGULAR((3,)),
            dma((2,)),
            dma((2,)),
            dma, dma, dma((2,)), dma((2,)), dma, dma, dma, dma, dma, dma, dma, dma,
        ],
        compiler_params=pltpu.CompilerParams(collective_id=0, has_side_effects=True, vmem_limit_bytes=40 * 1024 * 1024),
    )(factor, spectrum, psi, guess_scale, lag_cutoff, jnp.asarray(to_lag), jnp.asarray(to_freq))
    return jnp.swapaxes(out, 2, 3)


def solution(mesh):
    in_specs = (P("freq", None, "chan", None), P("freq", None, "chan", None), P("freq"), P())
    out_specs = P("freq", None, None, "chan")
    return jax.shard_map(step, mesh=mesh, in_specs=in_specs, out_specs=out_specs, check_vma=False)
```

```python
import functools

import jax
import jax.numpy as jnp
import numpy as np
from jax import lax
from jax.experimental import pallas as pl
from jax.experimental.pallas import tpu as pltpu
from jax.sharding import PartitionSpec as P

ITERS = 8
LOGICAL = pl.DeviceIdType.LOGICAL
BF = jnp.bfloat16
F32 = jnp.float32
C = 128
PANEL = 32
FL = 8
OWN = 2
G = 64
F = 512
LAGS = 256
VMEM_LIMIT = 67043328 - 1024 * 1024
Z_ORDER = (4, 3, 5, 2, 6, 1, 7, 0)
XY_ORDER = (2, 1, 3, 0)


def rem(a, b):
    return lax.rem(a, jnp.int32(b))


def div(a, b):
    return lax.div(a, jnp.int32(b))


def coords():
    f = lax.axis_index("freq")
    c = lax.axis_index("chan")
    return div(f, 16), rem(f, 4), div(c, 2) * 4 + rem(div(f, 4), 4), rem(c, 2)


def split(value):
    high = value.astype(BF)
    return high, (value - high.astype(F32)).astype(BF)


def embed(value):
    re, im = value[:, :C], value[:, C:]
    return jnp.concatenate([value, jnp.concatenate([-im, re], axis=1)], axis=0)


def dot(left, right):
    return jnp.dot(left, right, preferred_element_type=F32)


def dot_nt(left, right):
    return lax.dot_general(left, right, (((1,), (1,)), ((), ())), preferred_element_type=F32)


def dot_tn(left, right):
    return lax.dot_general(left, right, (((0,), (0,)), ((), ())), preferred_element_type=F32)


def dot_tt(left, right):
    return lax.dot_general(left, right, (((0,), (1,)), ((), ())), preferred_element_type=F32)


def tables():
    lag = np.arange(LAGS)[:, None]
    freq = np.arange(F)[None, :]
    angle = 2.0 * np.pi * ((lag * freq) % F) / F
    cos, sin = np.cos(angle), np.sin(angle)
    to_lag = np.concatenate([cos, sin], axis=1) / F
    to_freq = np.concatenate([cos.T, -sin.T], axis=1)

    def halves(table):
        high = table.astype(jnp.bfloat16)
        low = (table - high.astype(np.float64)).astype(jnp.bfloat16)
        return np.concatenate([high, low], axis=0)

    return halves(to_lag), halves(to_freq)


def turn(value, lane):
    ahead = pltpu.roll(value, 96, 1)
    behind = pltpu.roll(value, 32, 1)
    return jnp.where(rem(lane, 64) < 32, -ahead, behind)


def table_apply(table_ref, rows, value, lane):
    high, low = split(value)
    turn_high, turn_low = turn(value, lane), None
    turn_high, turn_low = split(turn_high)
    both = jnp.concatenate(
        [jnp.concatenate([high, low], axis=1), jnp.concatenate([turn_high, turn_low], axis=1)], axis=0
    )
    first = dot(table_ref[0:rows, :], both)
    second = dot(table_ref[rows : 2 * rows, :], jnp.concatenate([high, turn_high], axis=0))
    return first[:, :C] + first[:, C:] + second


def kernel(
    factor_ref, spectrum_ref, scale_ref, cutoff_ref, to_lag_hbm, to_freq_hbm, out_ref,
    spec_all, psi_all, send_f, recv_f, send_r, recv_r, to_lag, to_freq, stage_sem, local_sem, send_sem, recv_sem,
):
    x, y, z, k = coords()
    me_f = lax.axis_index("freq")
    me_c = lax.axis_index("chan")
    me_lin = me_f * 4 + me_c
    z_hi = div(z, 4)

    xs = [rem(x + i, 4) for i in range(4)]
    ys = [rem(y + i, 4) for i in range(4)]
    zs = [rem(z + i, 8) for i in range(8)]
    x_part = [v * 64 for v in xs]
    y_part = [v * 4 for v in ys]
    z_part = [rem(v, 4) * 16 + div(v, 4) * 2 for v in zs]
    k_part = [k, 1 - k]
    x_slot = [v * 16 for v in xs]
    z_slot = [rem(v, 4) * 4 + div(v, 4) * 128 for v in zs]
    k_slot = [k * 64, 64 - k * 64]

    def number(dx, dy, dz, dk):
        return x_part[dx] + y_part[dy] + z_part[dz] + k_part[dk]

    on_y = [number(0, i, 0, 0) for i in (2, 1, 3)]
    on_z = [number(0, 0, i, 0) for i in Z_ORDER[:-1]]
    on_x = [number(i, 0, 0, 0) for i in (2, 1, 3)]
    sibling, across, diagonal = number(0, 0, 0, 1), number(0, 0, 4, 0), number(0, 0, 4, 1)
    sibling_c, across_c, diagonal_c = rem(sibling, 4), rem(across, 4), rem(diagonal, 4)

    def signal(sem, peers):
        for peer in peers:
            pl.semaphore_signal(sem, inc=1, device_id=peer, device_id_type=LOGICAL)

    def remote(src, dst, i, peer):
        return pltpu.make_async_remote_copy(
            src_ref=src, dst_ref=dst, send_sem=send_sem.at[i], recv_sem=recv_sem.at[i], device_id=peer, device_id_type=LOGICAL
        )

    def wait_bytes(ref, sem):
        pltpu.make_async_copy(ref, ref, sem).wait()

    barrier = pltpu.get_barrier_semaphore()
    first_peers = [diagonal] + on_z + on_x + on_y + [sibling]
    signal(barrier, first_peers)

    def panel_rows(chan):
        return pl.ds(pl.multiple_of(chan * PANEL, PANEL), PANEL)

    def own_freqs(chan):
        return pl.ds(OWN * chan, OWN)

    my_rows = panel_rows(me_c)
    own_copies = [
        pltpu.make_async_copy(factor_ref, psi_all.at[:, :, my_rows, :], local_sem.at[0]),
        pltpu.make_async_copy(spectrum_ref.at[own_freqs(me_c)], spec_all.at[:, :, my_rows, :], local_sem.at[1]),
    ]
    tables_in = [
        pltpu.make_async_copy(to_lag_hbm, to_lag, local_sem.at[2]),
        pltpu.make_async_copy(to_freq_hbm, to_freq, local_sem.at[3]),
    ]
    for copy in own_copies + tables_in:
        copy.start()

    pl.semaphore_wait(barrier, len(first_peers))
    partners = ((across, across_c), (diagonal, diagonal_c), (sibling, sibling_c))
    for peer, chan in partners:
        freqs = own_freqs(chan)
        remote(factor_ref.at[freqs], psi_all.at[freqs, :, my_rows, :], 0, peer).start()
    for peer, chan in partners:
        remote(spectrum_ref.at[own_freqs(chan)], spec_all.at[:, :, my_rows, :], 1, peer).start()
    here_half = pl.ds(4 * z_hi, 4)
    there_half = pl.ds(4 - 4 * z_hi, 4)
    there_rows = pl.ds(pl.multiple_of(64 - 64 * z_hi, 64), 64)
    mine = own_freqs(me_c)
    later = [
        remote(factor_ref.at[here_half], psi_all.at[here_half, :, my_rows, :], 2, across),
        remote(factor_ref.at[there_half], psi_all.at[there_half, :, my_rows, :], 3, sibling),
        remote(factor_ref.at[mine], psi_all.at[mine, :, my_rows, :], 4, sibling),
    ]
    for copy in later:
        copy.start()
    signal(stage_sem.at[0], [sibling])
    pl.semaphore_wait(stage_sem.at[0], 1)
    signal(stage_sem.at[1], on_y)
    pl.semaphore_wait(stage_sem.at[1], 3)
    signal(stage_sem.at[2], on_z)

    own_copies[0].wait()
    wait_bytes(psi_all.at[pl.ds(0, OWN), :, pl.ds(0, 3 * PANEL), :], recv_sem.at[0])
    got = psi_all.at[mine, :, there_rows, :]
    relay_own = remote(got, got, 5, sibling)
    relay_own.start()

    row = lax.broadcasted_iota(jnp.int32, (C, 2 * C), 0)
    col = lax.broadcasted_iota(jnp.int32, (C, 2 * C), 1)
    eye = (row == col).astype(F32)
    lane = lax.broadcasted_iota(jnp.int32, (G, C), 1)

    psis, rs, qs = [], [], []
    for b in range(OWN):
        psi = jnp.concatenate([psi_all[OWN * me_c + b, 0], psi_all[OWN * me_c + b, 1]], axis=1)
        wide = embed(psi)
        r = eye - scale_ref[OWN * me_c + b] * dot_nt(psi, wide)
        psis.append(wide)
        rs.append(r)
        qs.append(eye + r)

    for step in range(1, ITERS):
        for b in range(OWN):
            r_high, r_low = split(rs[b])
            q_high, q_low = split(qs[b])
            square_left = jnp.concatenate([r_high, r_low, r_high], axis=1)
            e_high, e_low = embed(r_high), embed(r_low)
            right = jnp.concatenate([e_high, e_high, e_low], axis=0)
            r_next = dot(square_left, right)
            rs[b] = r_next
            n_high, n_low = split(r_next)
            en_high, en_low = embed(n_high), embed(n_low)
            qs[b] = qs[b] + dot(
                jnp.concatenate([q_high, q_low, q_high], axis=1), jnp.concatenate([en_high, en_high, en_low], axis=0)
            )

    own_copies[1].wait()
    wait_bytes(spec_all.at[:, :, pl.ds(0, 3 * PANEL), :], recv_sem.at[1])

    for b in range(OWN):
        q_high, q_low = split(qs[b])
        zz = scale_ref[OWN * me_c + b] * dot(
            jnp.concatenate([q_high, q_low], axis=1), jnp.concatenate([psis[b], psis[b]], axis=0)
        )
        z_high, z_low = split(zz)
        spec = jnp.concatenate([spec_all[b, 0], spec_all[b, 1]], axis=1)
        u = dot(
            jnp.concatenate([spec, spec], axis=1), jnp.concatenate([embed(z_high), embed(z_low)], axis=0)
        )
        u_high, u_low = split(u)

        def upright(value):
            return jnp.concatenate([value[:, :C], -value[:, C:]], axis=0)

        zs_high, zs_low = upright(z_high), upright(z_low)
        eu_high, eu_low = embed(u_high), embed(u_low)
        mid = eye + dot_tn(
            jnp.concatenate([zs_high, zs_low, zs_high], axis=0), jnp.concatenate([eu_high, eu_high, eu_low], axis=0)
        )
        pieces = [mid[:G, :C], mid[:G, C:], mid[G:, :C], mid[G:, C:]]
        for j in range(4):
            rolled = []
            for i, piece in enumerate(pieces):
                shift = (32 * i - 32 * j) % C
                rolled.append(pltpu.roll(piece, shift, 1) if shift else piece)
            packed = jnp.where(
                lane < 64,
                jnp.where(lane < 32, rolled[0], rolled[1]),
                jnp.where(lane < 96, rolled[2], rolled[3]),
            )
            send_f[pl.ds(G * j, G), b, :] = packed

    pl.semaphore_wait(stage_sem.at[2], len(on_z))
    kept = pltpu.make_async_copy(send_f.at[me_c * G + me_f], recv_f.at[me_lin], local_sem.at[4])
    kept.start()
    for dx in XY_ORDER:
        for dy in XY_ORDER:
            for dk in (1, 0):
                for dz in Z_ORDER:
                    if (dx, dy, dz, dk) != (0, 0, 0, 0):
                        slot = x_slot[dx] + ys[dy] + z_slot[dz] + k_slot[dk]
                        remote(send_f.at[slot], recv_f.at[me_lin], 6, number(dx, dy, dz, dk)).start()

    got = psi_all.at[there_half, :, panel_rows(across_c), :]
    wait_bytes(got, recv_sem.at[2])
    relay_rest = remote(got, got, 7, sibling)
    relay_rest.start()

    for copy in tables_in:
        copy.wait()
    kept.wait()
    wait_bytes(recv_f.at[pl.ds(0, 4 * G - 1)], recv_sem.at[6])

    gathered = recv_f[...].reshape(F, C)
    lane_f = lax.broadcasted_iota(jnp.int32, (F, C), 1)
    lane_l = lax.broadcasted_iota(jnp.int32, (LAGS, C), 1)
    lag_row = lax.broadcasted_iota(jnp.int32, (LAGS, C), 0)
    keep = jnp.where(lag_row == 0, 0.5, jnp.where(lag_row <= cutoff_ref[0], 1.0, 0.0)).astype(F32)
    lags = table_apply(to_lag, LAGS, gathered, lane_f) * keep
    send_r[...] = table_apply(to_freq, F, lags, lane_l)

    me_eight = pl.ds(pl.multiple_of(me_f * FL, FL), FL)
    kept = pltpu.make_async_copy(send_r.at[me_eight, :], recv_r.at[me_eight, :], local_sem.at[5])
    kept.start()
    z_lo = rem(z, 4)
    zl = [rem(z_lo + i, 4) for i in range(4)]
    for dx in XY_ORDER:
        for dy in XY_ORDER:
            for dz in (3, 1, 2, 0):
                if (dx, dy, dz) != (0, 0, 0):
                    other = x_slot[dx] + zl[dz] * 4 + ys[dy]
                    eight = pl.ds(pl.multiple_of(other * FL, FL), FL)
                    remote(send_r.at[eight, :], recv_r.at[me_eight, :], 8, other * 4 + me_c).start()

    later[1].wait_recv()
    later[2].wait_recv()
    relay_own.wait_recv()
    relay_rest.wait_recv()
    kept.wait()
    wait_bytes(recv_r.at[pl.ds(0, F - FL), :], recv_sem.at[8])

    for f in range(FL):
        d = recv_r[pl.ds(f, G, stride=FL), :]
        high, low = split(d)
        stack = jnp.concatenate(
            [
                jnp.concatenate([high[:, :64], low[:, :64]], axis=1),
                jnp.concatenate([high[:, 64:], low[:, 64:]], axis=1),
            ],
            axis=0,
        )
        both = jnp.concatenate([psi_all[f, 0], psi_all[f, 1]], axis=0)
        got = dot_tt(stack, both)
        got = got[:64] + got[64:]
        out_ref[f, 0] = got[:32, :C] - got[32:, C:]
        out_ref[f, 1] = got[32:, :C] + got[:32, C:]

    wait_bytes(psi_all.at[pl.ds(0, OWN), :, pl.ds(0, 3 * PANEL), :], send_sem.at[0])
    wait_bytes(spec_all.at[:, :, pl.ds(0, 3 * PANEL), :], send_sem.at[1])
    for copy in later + [relay_own, relay_rest]:
        copy.wait_send()
    wait_bytes(send_f.at[pl.ds(0, 4 * G - 1)], send_sem.at[6])
    wait_bytes(send_r.at[pl.ds(0, F - FL), :], send_sem.at[8])


def step(factor, spectrum, guess_scale, lag_cutoff):
    to_lag, to_freq = tables()
    vmem = pl.BlockSpec(memory_space=pltpu.VMEM)
    smem = pl.BlockSpec(memory_space=pltpu.SMEM)
    hbm = pl.BlockSpec(memory_space=pltpu.HBM)
    dma = pltpu.SemaphoreType.DMA
    out = pl.pallas_call(
        kernel,
        out_shape=jax.ShapeDtypeStruct((FL, 2, PANEL, C), F32),
        in_specs=[hbm, hbm, smem, smem, hbm, hbm],
        out_specs=vmem,
        scratch_shapes=[
            pltpu.VMEM((OWN, 2, C, C), BF),
            pltpu.VMEM((FL, 2, C, C), BF),
            pltpu.VMEM((4 * G, OWN, C), F32),
            pltpu.VMEM((4 * G, OWN, C), F32),
            pltpu.VMEM((F, C), F32),
            pltpu.VMEM((F, C), F32),
            pltpu.VMEM(to_lag.shape, BF),
            pltpu.VMEM(to_freq.shape, BF),
            pltpu.SemaphoreType.REGULAR((3,)),
            dma((6,)),
            dma((9,)),
            dma((9,)),
        ],
        compiler_params=pltpu.CompilerParams(collective_id=0, has_side_effects=True, vmem_limit_bytes=VMEM_LIMIT),
    )(factor, spectrum, guess_scale, lag_cutoff, jnp.asarray(to_lag), jnp.asarray(to_freq))
    return jnp.swapaxes(out, 2, 3)


def solution(mesh):
    in_specs = (P("freq", None, "chan", None), P("freq", None, "chan", None), P("freq"), P())
    out_specs = P("freq", None, None, "chan")
    return jax.shard_map(step, mesh=mesh, in_specs=in_specs, out_specs=out_specs, check_vma=False)
```

```python
import math

import jax
import jax.numpy as jnp
import numpy as np
from jax import lax
from jax.experimental import pallas as pl
from jax.experimental.pallas import tpu as pltpu
from jax.sharding import PartitionSpec as P

ITERS = 8
LOGICAL = pl.DeviceIdType.LOGICAL
BF = jnp.bfloat16
F32 = jnp.float32
C = 128
PANEL = 32
FL = 8
OWN = 2
G = 64
F = 512
LAGS = 256
FLOOR = 2.0**-16
STEPS = 32767 / (40 * math.log(2.0))
VMEM_LIMIT = 67043328 - 1024 * 1024
Z_ORDER = (4, 3, 5, 2, 6, 1, 7, 0)
XY_ORDER = (2, 1, 3, 0)


def rem(a, b):
    return lax.rem(a, jnp.int32(b))


def div(a, b):
    return lax.div(a, jnp.int32(b))


def coords():
    f = lax.axis_index("freq")
    c = lax.axis_index("chan")
    return div(f, 16), rem(f, 4), div(c, 2) * 4 + rem(div(f, 4), 4), rem(c, 2)


def split(value):
    high = value.astype(BF)
    return high, (value - high.astype(F32)).astype(BF)


def embed(value):
    re, im = value[:, :C], value[:, C:]
    return jnp.concatenate([value, jnp.concatenate([-im, re], axis=1)], axis=0)


def code(value):
    steps = jnp.minimum(jnp.log(1.0 + jnp.abs(value) * (1.0 / FLOOR)) * STEPS + 0.5, 32767.0).astype(jnp.int32)
    return jnp.where(value < 0, -steps, steps)


def decode(number):
    value = number.astype(F32)
    size = FLOOR * jnp.exp(jnp.abs(value) * (1.0 / STEPS)) - FLOOR
    return jnp.where(number < 0, -size, size)


def pack(low, high):
    return code(low) + (code(high) << 16)


def unpack(word):
    low = (word << 16) >> 16
    return decode(low), decode((word - low) >> 16)


def dot(left, right):
    return jnp.dot(left, right, preferred_element_type=F32)


def dot_nt(left, right):
    return lax.dot_general(left, right, (((1,), (1,)), ((), ())), preferred_element_type=F32)


def dot_tn(left, right):
    return lax.dot_general(left, right, (((0,), (0,)), ((), ())), preferred_element_type=F32)


def dot_tt(left, right):
    return lax.dot_general(left, right, (((0,), (1,)), ((), ())), preferred_element_type=F32)


def tables():
    to_lag, to_freq = [], []
    pairs = np.arange(C).reshape(C // 2, 2).T.reshape(-1)
    fours = np.arange(C).reshape(C // 8, 2, 4).swapaxes(0, 1).reshape(-1)
    for r in range(4):
        lag = 4 * np.arange(LAGS // 4) + r
        angle = 2.0 * np.pi * (np.outer(lag, pairs) % F) / F
        to_lag.append(np.concatenate([np.cos(angle), np.sin(angle)], axis=0) / F)
        angle = 2.0 * np.pi * (np.outer(lag, fours) % F) / F
        to_freq.append(np.concatenate([np.cos(angle).T, -np.sin(angle).T], axis=1))
    table = np.concatenate(to_lag + to_freq, axis=0)
    high = table.astype(jnp.bfloat16)
    low = (table - high.astype(np.float64)).astype(jnp.bfloat16)
    return np.concatenate([high, low], axis=0)


def turn(value):
    lane = lax.broadcasted_iota(jnp.int32, value.shape, 1)
    return jnp.where(rem(lane, 64) < 32, -pltpu.roll(value, 96, 1), pltpu.roll(value, 32, 1))


def table_dot(table_ref, block, value):
    high, low = split(value)
    first = dot(table_ref[pl.ds(C * block, C), :], jnp.concatenate([high, low], axis=1))
    return first[:, :C] + first[:, C:] + dot(table_ref[pl.ds(C * (block + 8), C), :], high)


def project(table_ref, m, cutoff):
    even, odd, even_d, odd_d = m[0] + m[2], m[1] + m[3], m[0] - m[2], turn(m[1] - m[3])
    sums = [even + odd, even_d + odd_d, even - odd, even_d - odd_d]
    row = lax.broadcasted_iota(jnp.int32, (LAGS // 4, C), 0)
    back = []
    for r in range(4):
        both = table_dot(table_ref, r, sums[r])
        lag = 4 * row + r
        keep = jnp.where(lag == 0, 0.5, jnp.where(lag <= cutoff, 1.0, 0.0)).astype(F32)
        lags = (both[: LAGS // 4] + turn(both[LAGS // 4 :])) * keep
        back.append(table_dot(table_ref, 4 + r, jnp.concatenate([lags, turn(lags)], axis=0)))
    even, odd, even_d, odd_d = back[0] + back[2], back[1] + back[3], back[0] - back[2], turn(back[1] - back[3])
    return [even + odd, even_d - odd_d, even - odd, even_d + odd_d]


def kernel(
    factor_ref, spectrum_ref, scale_hbm, cutoff_ref, table_hbm, out_ref,
    spec_all, psi_all, send_f, recv_f, send_r, recv_r, table, scale_ref, stage_sem, local_sem, send_sem, recv_sem,
):
    x, y, z, k = coords()
    me_f = lax.axis_index("freq")
    me_c = lax.axis_index("chan")
    me_lin = me_f * 4 + me_c
    z_hi = div(me_c, 2)

    def wrapped(value, size):
        return [value] + [value + i - jnp.where(value >= size - i, size, 0) for i in range(1, size)]

    xs, ys, zs = wrapped(x, 4), wrapped(y, 4), wrapped(z, 8)
    zh = [jnp.where(v >= 4, 1, 0) for v in zs]
    x_part = [v * 64 for v in xs]
    y_part = [v * 4 for v in ys]
    z_part = [v * 16 - h * 62 for v, h in zip(zs, zh)]
    k_part = [k, 1 - k]
    x_slot = [v * 16 for v in xs]
    z_slot = [v * 4 + h * 112 for v, h in zip(zs, zh)]
    k_slot = [k * 64, 64 - k * 64]

    def number(dx, dy, dz, dk):
        return x_part[dx] + y_part[dy] + z_part[dz] + k_part[dk]

    on_y = [number(0, i, 0, 0) for i in (2, 1, 3)]
    on_z = [number(0, 0, i, 0) for i in Z_ORDER[:-1]]
    on_x = [number(i, 0, 0, 0) for i in (2, 1, 3)]
    sibling, across, diagonal = number(0, 0, 0, 1), number(0, 0, 4, 0), number(0, 0, 4, 1)
    sibling_c = 2 * z_hi + 1 - k
    across_c = 2 - 2 * z_hi + k
    diagonal_c = 3 - 2 * z_hi - k

    def signal(sem, peers):
        for peer in peers:
            pl.semaphore_signal(sem, inc=1, device_id=peer, device_id_type=LOGICAL)

    def remote(src, dst, i, peer):
        return pltpu.make_async_remote_copy(
            src_ref=src, dst_ref=dst, send_sem=send_sem.at[i], recv_sem=recv_sem.at[i], device_id=peer, device_id_type=LOGICAL
        )

    def wait_bytes(ref, sem):
        pltpu.make_async_copy(ref, ref, sem).wait()

    barrier = pltpu.get_barrier_semaphore()
    first_peers = [diagonal] + on_z + on_x + on_y + [sibling]
    signal(barrier, first_peers)

    def panel_rows(chan):
        return pl.ds(pl.multiple_of(chan * PANEL, PANEL), PANEL)

    def own_freqs(chan):
        return pl.ds(OWN * chan, OWN)

    my_rows = panel_rows(me_c)
    own_copies = [
        pltpu.make_async_copy(factor_ref, psi_all.at[:, :, my_rows, :], local_sem.at[0]),
        pltpu.make_async_copy(spectrum_ref.at[own_freqs(me_c)], spec_all.at[:, :, my_rows, :], local_sem.at[1]),
    ]
    scale_in = pltpu.make_async_copy(scale_hbm, scale_ref, local_sem.at[2])
    table_in = pltpu.make_async_copy(table_hbm, table, local_sem.at[3])
    for copy in own_copies + [scale_in, table_in]:
        copy.start()

    pl.semaphore_wait(barrier, len(first_peers))
    partners = ((across, across_c), (diagonal, diagonal_c), (sibling, sibling_c))
    for peer, chan in partners:
        freqs = own_freqs(chan)
        remote(factor_ref.at[freqs], psi_all.at[freqs, :, my_rows, :], 0, peer).start()
    for peer, chan in partners:
        remote(spectrum_ref.at[own_freqs(chan)], spec_all.at[:, :, my_rows, :], 1, peer).start()
    here_half = pl.ds(4 * z_hi, 4)
    there_half = pl.ds(4 - 4 * z_hi, 4)
    there_rows = pl.ds(pl.multiple_of(64 - 64 * z_hi, 64), 64)
    mine = own_freqs(me_c)
    later = [
        remote(factor_ref.at[here_half], psi_all.at[here_half, :, my_rows, :], 2, across),
        remote(factor_ref.at[there_half], psi_all.at[there_half, :, my_rows, :], 3, sibling),
        remote(factor_ref.at[mine], psi_all.at[mine, :, my_rows, :], 4, sibling),
    ]
    for copy in later:
        copy.start()
    signal(stage_sem.at[0], [sibling])
    pl.semaphore_wait(stage_sem.at[0], 1)
    signal(stage_sem.at[1], on_y)
    pl.semaphore_wait(stage_sem.at[1], 3)
    signal(stage_sem.at[2], on_z)

    own_copies[0].wait()
    scale_in.wait()
    wait_bytes(psi_all.at[pl.ds(0, OWN), :, pl.ds(0, 3 * PANEL), :], recv_sem.at[0])
    got = psi_all.at[mine, :, there_rows, :]
    relay_own = remote(got, got, 5, sibling)
    relay_own.start()

    row = lax.broadcasted_iota(jnp.int32, (C, 2 * C), 0)
    col = lax.broadcasted_iota(jnp.int32, (C, 2 * C), 1)
    eye = (row == col).astype(F32)
    lane = lax.broadcasted_iota(jnp.int32, (G, C), 1)

    psis, rs, qs = [], [], []
    for b in range(OWN):
        psi = jnp.concatenate([psi_all[OWN * me_c + b, 0], psi_all[OWN * me_c + b, 1]], axis=1)
        wide = embed(psi)
        r = eye - scale_ref[OWN * me_c + b] * dot_nt(psi, wide)
        psis.append(wide)
        rs.append(r)
        qs.append(eye + r)

    for step in range(1, ITERS):
        for b in range(OWN):
            r_high, r_low = split(rs[b])
            q_high, q_low = split(qs[b])
            square_left = jnp.concatenate([r_high, r_low, r_high], axis=1)
            e_high, e_low = embed(r_high), embed(r_low)
            right = jnp.concatenate([e_high, e_high, e_low], axis=0)
            r_next = dot(square_left, right)
            rs[b] = r_next
            n_high, n_low = split(r_next)
            en_high, en_low = embed(n_high), embed(n_low)
            qs[b] = qs[b] + dot(
                jnp.concatenate([q_high, q_low, q_high], axis=1), jnp.concatenate([en_high, en_high, en_low], axis=0)
            )

    own_copies[1].wait()
    wait_bytes(spec_all.at[:, :, pl.ds(0, 3 * PANEL), :], recv_sem.at[1])

    def upright(value):
        return jnp.concatenate([value[:, :C], -value[:, C:]], axis=0)

    specs = [jnp.concatenate([spec_all[b, 0], spec_all[b, 1]], axis=1) for b in range(OWN)]
    zs_split, us_split = [], []
    for b in range(OWN):
        q_high, q_low = split(qs[b])
        zz = dot(jnp.concatenate([q_high, q_low], axis=1), jnp.concatenate([psis[b], psis[b]], axis=0))
        zs_split.append(split(scale_ref[OWN * me_c + b] * zz))
    for b in range(OWN):
        z_high, z_low = zs_split[b]
        u = dot(
            jnp.concatenate([specs[b], specs[b]], axis=1), jnp.concatenate([embed(z_high), embed(z_low)], axis=0)
        )
        us_split.append(split(u))
    mids = []
    for b in range(OWN):
        zs_high, zs_low = upright(zs_split[b][0]), upright(zs_split[b][1])
        eu_high, eu_low = embed(us_split[b][0]), embed(us_split[b][1])
        mids.append(
            eye
            + dot_tn(
                jnp.concatenate([zs_high, zs_low, zs_high], axis=0), jnp.concatenate([eu_high, eu_high, eu_low], axis=0)
            )
        )
    half = C // 2
    words = [pack(mids[0][:, :C], mids[1][:, :C]), pack(mids[0][:, C:], mids[1][:, C:])]
    pieces = [words[0][:half], words[1][:half], words[0][half:], words[1][half:]]
    for j in range(4):
        rolled = []
        for i, piece in enumerate(pieces):
            shift = (32 * i - 32 * j) % C
            rolled.append(pltpu.roll(piece, shift, 1) if shift else piece)
        send_f[pl.ds(G * j, G), 0, :] = jnp.where(
            lane < 64,
            jnp.where(lane < 32, rolled[0], rolled[1]),
            jnp.where(lane < 96, rolled[2], rolled[3]),
        )

    pl.semaphore_wait(stage_sem.at[2], len(on_z))
    kept = pltpu.make_async_copy(send_f.at[me_c * G + me_f], recv_f.at[me_lin], local_sem.at[4])
    kept.start()
    for dx in XY_ORDER:
        for dy in XY_ORDER:
            for dk in (1, 0):
                for dz in Z_ORDER:
                    if (dx, dy, dz, dk) != (0, 0, 0, 0):
                        slot = x_slot[dx] + ys[dy] + z_slot[dz] + k_slot[dk]
                        remote(send_f.at[slot], recv_f.at[me_lin], 6, number(dx, dy, dz, dk)).start()

    got = psi_all.at[there_half, :, panel_rows(across_c), :]
    wait_bytes(got, recv_sem.at[2])
    relay_rest = remote(got, got, 7, sibling)
    relay_rest.start()

    table_in.wait()
    kept.wait()
    wait_bytes(recv_f.at[pl.ds(0, 4 * G - 1)], recv_sem.at[6])

    even, odd = unpack(recv_f[...].reshape(4 * G, C))
    blocks = [jnp.concatenate([even[G * i : G * (i + 1)], odd[G * i : G * (i + 1)]], axis=0) for i in range(4)]
    parts = project(table, blocks, cutoff_ref[0])
    for i in range(4):
        send_r[pl.ds(G // 4 * i, G // 4)] = pack(parts[i][:G], parts[i][G:]).reshape(G // 4, 4, C)

    kept = pltpu.make_async_copy(send_r.at[me_f], recv_r.at[me_f], local_sem.at[5])
    kept.start()
    zl = wrapped(z - 4 * z_hi, 4)
    for dx in XY_ORDER:
        for dy in XY_ORDER:
            for dz in (3, 1, 2, 0):
                if (dx, dy, dz) != (0, 0, 0):
                    other = x_slot[dx] + zl[dz] * 4 + ys[dy]
                    remote(send_r.at[other], recv_r.at[me_f], 8, other * 4 + me_c).start()

    later[1].wait_recv()
    later[2].wait_recv()
    relay_own.wait_recv()
    relay_rest.wait_recv()
    kept.wait()
    wait_bytes(recv_r.at[pl.ds(0, G - 1)], recv_sem.at[8])

    causal = [unpack(recv_r[:, f, :]) for f in range(4)]
    for f in range(FL):
        high, low = split(causal[f % 4][f // 4])
        stack = jnp.concatenate(
            [
                jnp.concatenate([high[:, :64], low[:, :64]], axis=1),
                jnp.concatenate([high[:, 64:], low[:, 64:]], axis=1),
            ],
            axis=0,
        )
        both = jnp.concatenate([psi_all[f, 0], psi_all[f, 1]], axis=0)
        got = dot_tt(stack, both)
        got = got[:64] + got[64:]
        out_ref[f, 0] = got[:32, :C] - got[32:, C:]
        out_ref[f, 1] = got[32:, :C] + got[:32, C:]

    wait_bytes(psi_all.at[pl.ds(0, OWN), :, pl.ds(0, 3 * PANEL), :], send_sem.at[0])
    wait_bytes(spec_all.at[:, :, pl.ds(0, 3 * PANEL), :], send_sem.at[1])
    for copy in later + [relay_own, relay_rest]:
        copy.wait_send()
    wait_bytes(send_f.at[pl.ds(0, 4 * G - 1)], send_sem.at[6])
    wait_bytes(send_r.at[pl.ds(0, G - 1)], send_sem.at[8])


def step(factor, spectrum, guess_scale, lag_cutoff):
    table = tables()
    vmem = pl.BlockSpec(memory_space=pltpu.VMEM)
    smem = pl.BlockSpec(memory_space=pltpu.SMEM)
    hbm = pl.BlockSpec(memory_space=pltpu.HBM)
    dma = pltpu.SemaphoreType.DMA
    out = pl.pallas_call(
        kernel,
        out_shape=jax.ShapeDtypeStruct((FL, 2, PANEL, C), F32),
        in_specs=[hbm, hbm, hbm, smem, hbm],
        out_specs=vmem,
        scratch_shapes=[
            pltpu.VMEM((OWN, 2, C, C), BF),
            pltpu.VMEM((FL, 2, C, C), BF),
            pltpu.VMEM((4 * G, 1, C), jnp.int32),
            pltpu.VMEM((4 * G, 1, C), jnp.int32),
            pltpu.VMEM((G, 4, C), jnp.int32),
            pltpu.VMEM((G, 4, C), jnp.int32),
            pltpu.VMEM(table.shape, BF),
            pltpu.SMEM((FL,), F32),
            pltpu.SemaphoreType.REGULAR((3,)),
            dma((6,)),
            dma((9,)),
            dma((9,)),
        ],
        compiler_params=pltpu.CompilerParams(collective_id=0, has_side_effects=True, vmem_limit_bytes=VMEM_LIMIT),
    )(factor, spectrum, guess_scale, lag_cutoff, jnp.asarray(table))
    return jnp.swapaxes(out, 2, 3)


def solution(mesh):
    in_specs = (P("freq", None, "chan", None), P("freq", None, "chan", None), P("freq"), P())
    out_specs = P("freq", None, None, "chan")
    return jax.shard_map(step, mesh=mesh, in_specs=in_specs, out_specs=out_specs, check_vma=False)
```

```python
import math

import jax
import jax.numpy as jnp
import numpy as np
from jax import lax
from jax.experimental import pallas as pl
from jax.experimental.pallas import tpu as pltpu
from jax.sharding import PartitionSpec as P

ITERS = 8
LOGICAL = pl.DeviceIdType.LOGICAL
BF = jnp.bfloat16
F32 = jnp.float32
C = 128
PANEL = 32
FL = 8
OWN = 2
G = 64
F = 512
LAGS = 256
FLOOR = 2.0**-16
STEPS = 32767 / (40 * math.log(2.0))
VMEM_LIMIT = 67043328 - 11000 * 1024
Z_ORDER = (4, 3, 5, 2, 6, 1, 7, 0)
XY_ORDER = (2, 1, 3, 0)


def rem(a, b):
    return lax.rem(a, jnp.int32(b))


def div(a, b):
    return lax.div(a, jnp.int32(b))


def coords():
    f = lax.axis_index("freq")
    c = lax.axis_index("chan")
    return div(f, 16), rem(f, 4), div(c, 2) * 4 + rem(div(f, 4), 4), rem(c, 2)


def split(value):
    high = value.astype(BF)
    return high, (value - high.astype(F32)).astype(BF)


def embed(value):
    re, im = value[:, :C], value[:, C:]
    return jnp.concatenate([value, jnp.concatenate([-im, re], axis=1)], axis=0)


def code(value):
    steps = jnp.minimum(jnp.log(1.0 + jnp.abs(value) * (1.0 / FLOOR)) * STEPS + 0.5, 32767.0).astype(jnp.int32)
    return jnp.where(value < 0, -steps, steps)


def decode(number):
    value = number.astype(F32)
    size = FLOOR * jnp.exp(jnp.abs(value) * (1.0 / STEPS)) - FLOOR
    return jnp.where(number < 0, -size, size)


def pack(low, high):
    return code(low) + (code(high) << 16)


def unpack(word):
    low = (word << 16) >> 16
    return decode(low), decode((word - low) >> 16)


def dot(left, right):
    return jnp.dot(left, right, preferred_element_type=F32)


def dot_nt(left, right):
    return lax.dot_general(left, right, (((1,), (1,)), ((), ())), preferred_element_type=F32)


def dot_tn(left, right):
    return lax.dot_general(left, right, (((0,), (0,)), ((), ())), preferred_element_type=F32)


def dot_tt(left, right):
    return lax.dot_general(left, right, (((0,), (1,)), ((), ())), preferred_element_type=F32)


def tables():
    to_lag, to_freq = [], []
    pairs = np.arange(C).reshape(C // 2, 2).T.reshape(-1)
    fours = np.arange(C).reshape(C // 8, 2, 4).swapaxes(0, 1).reshape(-1)
    for r in range(4):
        lag = 4 * np.arange(LAGS // 4) + r
        angle = 2.0 * np.pi * (np.outer(lag, pairs) % F) / F
        to_lag.append(np.concatenate([np.cos(angle), np.sin(angle)], axis=0) / F)
        angle = 2.0 * np.pi * (np.outer(lag, fours) % F) / F
        to_freq.append(np.concatenate([np.cos(angle).T, -np.sin(angle).T], axis=1))
    table = np.concatenate(to_lag + to_freq, axis=0)
    high = table.astype(jnp.bfloat16)
    low = (table - high.astype(np.float64)).astype(jnp.bfloat16)
    return np.concatenate([high, low], axis=0)


def turn(value):
    lane = lax.broadcasted_iota(jnp.int32, value.shape, 1)
    return jnp.where(rem(lane, 64) < 32, -pltpu.roll(value, 96, 1), pltpu.roll(value, 32, 1))


def table_dot(table_ref, block, value):
    high, low = split(value)
    first = dot(table_ref[pl.ds(C * block, C), :], jnp.concatenate([high, low], axis=1))
    return first[:, :C] + first[:, C:] + dot(table_ref[pl.ds(C * (block + 8), C), :], high)


def project(table_ref, m, cutoff):
    even, odd, even_d, odd_d = m[0] + m[2], m[1] + m[3], m[0] - m[2], turn(m[1] - m[3])
    sums = [even + odd, even_d + odd_d, even - odd, even_d - odd_d]
    row = lax.broadcasted_iota(jnp.int32, (LAGS // 4, C), 0)
    back = []
    for r in range(4):
        both = table_dot(table_ref, r, sums[r])
        lag = 4 * row + r
        keep = jnp.where(lag == 0, 0.5, jnp.where(lag <= cutoff, 1.0, 0.0)).astype(F32)
        lags = (both[: LAGS // 4] + turn(both[LAGS // 4 :])) * keep
        back.append(table_dot(table_ref, 4 + r, jnp.concatenate([lags, turn(lags)], axis=0)))
    even, odd, even_d, odd_d = back[0] + back[2], back[1] + back[3], back[0] - back[2], turn(back[1] - back[3])
    return [even + odd, even_d - odd_d, even - odd, even_d + odd_d]


def kernel(
    factor_ref, spectrum_ref, scale_hbm, cutoff_ref, table_hbm, out_ref,
    spec_all, psi_all, send_f, recv_f, send_r, recv_r, table, scale_ref, stage_sem, local_sem, send_sem, recv_sem,
):
    x, y, z, k = coords()
    me_f = lax.axis_index("freq")
    me_c = lax.axis_index("chan")
    me_lin = me_f * 4 + me_c
    z_hi = div(me_c, 2)

    def wrapped(value, size):
        return [value] + [value + i - jnp.where(value >= size - i, size, 0) for i in range(1, size)]

    xs, ys, zs = wrapped(x, 4), wrapped(y, 4), wrapped(z, 8)
    zh = [jnp.where(v >= 4, 1, 0) for v in zs]
    x_part = [v * 64 for v in xs]
    y_part = [v * 4 for v in ys]
    z_part = [v * 16 - h * 62 for v, h in zip(zs, zh)]
    k_part = [k, 1 - k]

    def number(dx, dy, dz, dk):
        return x_part[dx] + y_part[dy] + z_part[dz] + k_part[dk]

    on_y = [number(0, i, 0, 0) for i in (2, 1, 3)]
    on_z = [number(0, 0, i, 0) for i in Z_ORDER[:-1]]
    on_x = [number(i, 0, 0, 0) for i in (2, 1, 3)]
    sibling, across, diagonal = number(0, 0, 0, 1), number(0, 0, 4, 0), number(0, 0, 4, 1)
    sibling_c = 2 * z_hi + 1 - k
    across_c = 2 - 2 * z_hi + k
    diagonal_c = 3 - 2 * z_hi - k

    def signal(sem, peers):
        for peer in peers:
            pl.semaphore_signal(sem, inc=1, device_id=peer, device_id_type=LOGICAL)

    def remote(src, dst, i, peer):
        return pltpu.make_async_remote_copy(
            src_ref=src, dst_ref=dst, send_sem=send_sem.at[i], recv_sem=recv_sem.at[i], device_id=peer, device_id_type=LOGICAL
        )

    def wait_bytes(ref, sem):
        pltpu.make_async_copy(ref, ref, sem).wait()

    barrier = pltpu.get_barrier_semaphore()
    first_peers = [diagonal] + on_z + on_x + on_y + [sibling]
    signal(barrier, first_peers)

    def panel_rows(chan):
        return pl.ds(pl.multiple_of(chan * PANEL, PANEL), PANEL)

    def own_freqs(chan):
        return pl.ds(OWN * chan, OWN)

    my_rows = panel_rows(me_c)
    own_copies = [
        pltpu.make_async_copy(factor_ref, psi_all.at[:, :, my_rows, :], local_sem.at[0]),
        pltpu.make_async_copy(spectrum_ref.at[own_freqs(me_c)], spec_all.at[:, :, my_rows, :], local_sem.at[1]),
    ]
    scale_in = pltpu.make_async_copy(scale_hbm, scale_ref, local_sem.at[2])
    table_in = pltpu.make_async_copy(table_hbm, table, local_sem.at[3])
    for copy in own_copies + [scale_in, table_in]:
        copy.start()

    pl.semaphore_wait(barrier, len(first_peers))
    partners = ((across, across_c), (diagonal, diagonal_c), (sibling, sibling_c))
    for peer, chan in partners:
        freqs = own_freqs(chan)
        remote(factor_ref.at[freqs], psi_all.at[freqs, :, my_rows, :], 0, peer).start()
    for peer, chan in partners:
        remote(spectrum_ref.at[own_freqs(chan)], spec_all.at[:, :, my_rows, :], 1, peer).start()
    mine = own_freqs(me_c)
    here_half = pl.ds(4 * z_hi, 4)
    there_half = pl.ds(4 - 4 * z_hi, 4)
    later = [
        remote(factor_ref.at[here_half], psi_all.at[here_half, :, my_rows, :], 2, across),
        remote(factor_ref.at[there_half], psi_all.at[there_half, :, my_rows, :], 3, sibling),
        remote(factor_ref.at[mine], psi_all.at[mine, :, my_rows, :], 4, sibling),
    ]
    for copy in later:
        copy.start()

    signal(stage_sem.at[0], [sibling])
    pl.semaphore_wait(stage_sem.at[0], 1)
    signal(stage_sem.at[1], on_y)
    pl.semaphore_wait(stage_sem.at[1], 3)
    signal(stage_sem.at[2], on_z)

    own_copies[0].wait()
    scale_in.wait()
    wait_bytes(psi_all.at[pl.ds(0, OWN), :, pl.ds(0, 3 * PANEL), :], recv_sem.at[0])
    there_rows = pl.ds(pl.multiple_of(64 - 64 * z_hi, 64), 64)
    got = psi_all.at[mine, :, there_rows, :]
    relay_own = remote(got, got, 5, sibling)
    relay_own.start()

    row = lax.broadcasted_iota(jnp.int32, (C, 2 * C), 0)
    col = lax.broadcasted_iota(jnp.int32, (C, 2 * C), 1)
    eye = (row == col).astype(F32)
    lane = lax.broadcasted_iota(jnp.int32, (G, C), 1)

    psis, rs, qs = [], [], []
    for b in range(OWN):
        psi = jnp.concatenate([psi_all[OWN * me_c + b, 0], psi_all[OWN * me_c + b, 1]], axis=1)
        wide = embed(psi)
        r = eye - scale_ref[OWN * me_c + b] * dot_nt(psi, wide)
        psis.append(wide)
        rs.append(r)
        qs.append(eye + r)

    def times(left, right_high, right_low):
        high, low = split(left)
        e_high, e_low = embed(right_high), embed(right_low)
        rows = left.shape[0]
        most = dot(jnp.concatenate([high, low], axis=0), e_high)
        return most[:rows] + (most[rows:] + dot(high, e_low))

    for step in range(ITERS):
        for b in range(OWN):
            right = split(rs[b])
            if step == 0:
                rs[b] = times(rs[b], *right)
            elif step < ITERS - 1:
                both = times(jnp.concatenate([rs[b], qs[b]], axis=0), *right)
                rs[b] = both[:C]
                qs[b] = qs[b] + both[C:]
            else:
                qs[b] = qs[b] + times(qs[b], *right)

    def upright(value):
        return jnp.concatenate([value[:, :C], -value[:, C:]], axis=0)

    zs_split, us_split = [], []
    for b in range(OWN):
        q_high, q_low = split(qs[b])
        zz = dot(jnp.concatenate([q_high, q_low], axis=0), psis[b])
        zs_split.append(split(scale_ref[OWN * me_c + b] * (zz[:C] + zz[C:])))
    own_copies[1].wait()
    wait_bytes(spec_all.at[:, :, pl.ds(0, 3 * PANEL), :], recv_sem.at[1])
    for b in range(OWN):
        z_high, z_low = zs_split[b]
        spec = jnp.concatenate([spec_all[b, 0], spec_all[b, 1]], axis=1)
        u = dot(
            jnp.concatenate([spec, spec], axis=1), jnp.concatenate([embed(z_high), embed(z_low)], axis=0)
        )
        us_split.append(split(u))
    mids = []
    for b in range(OWN):
        zs_high, zs_low = upright(zs_split[b][0]), upright(zs_split[b][1])
        eu_high, eu_low = embed(us_split[b][0]), embed(us_split[b][1])
        mids.append(
            eye
            + dot_tn(
                jnp.concatenate([zs_high, zs_low, zs_high], axis=0), jnp.concatenate([eu_high, eu_high, eu_low], axis=0)
            )
        )
    half = C // 2
    words = [pack(mids[0][:, :C], mids[1][:, :C]), pack(mids[0][:, C:], mids[1][:, C:])]
    pieces = [words[0][:half], words[1][:half], words[0][half:], words[1][half:]]
    for j in range(4):
        rolled = []
        for i, piece in enumerate(pieces):
            shift = (32 * i - 32 * j) % C
            rolled.append(pltpu.roll(piece, shift, 1) if shift else piece)
        send_f[pl.ds(G * j, G), :] = jnp.where(
            lane < 64,
            jnp.where(lane < 32, rolled[0], rolled[1]),
            jnp.where(lane < 96, rolled[2], rolled[3]),
        )

    x_slot = [v * 16 for v in xs]
    z_slot = [v * 4 + h * 112 for v, h in zip(zs, zh)]
    k_slot = [k * 64, 64 - k * 64]
    pl.semaphore_wait(stage_sem.at[2], len(on_z))
    kept = pltpu.make_async_copy(send_f.at[pl.ds(me_c * G + me_f, 1)], recv_f.at[pl.ds(me_lin, 1)], local_sem.at[4])
    kept.start()
    for dx in XY_ORDER:
        for dy in XY_ORDER:
            for dk in (1, 0):
                for dz in Z_ORDER:
                    if (dx, dy, dz, dk) != (0, 0, 0, 0):
                        slot = x_slot[dx] + ys[dy] + z_slot[dz] + k_slot[dk]
                        remote(send_f.at[pl.ds(slot, 1)], recv_f.at[pl.ds(me_lin, 1)], 6, number(dx, dy, dz, dk)).start()

    got = psi_all.at[there_half, :, panel_rows(across_c), :]
    wait_bytes(got, recv_sem.at[2])
    relay_rest = remote(got, got, 7, sibling)
    relay_rest.start()

    table_in.wait()
    kept.wait()
    wait_bytes(recv_f.at[pl.ds(0, 4 * G - 1)], recv_sem.at[6])

    even, odd = unpack(recv_f[...])
    blocks = [jnp.concatenate([even[G * i : G * (i + 1)], odd[G * i : G * (i + 1)]], axis=0) for i in range(4)]
    parts = project(table, blocks, cutoff_ref[0])
    for i in range(4):
        send_r[pl.ds(G * i, G), :] = pack(parts[i][:G], parts[i][G:])

    me_four = pl.ds(pl.multiple_of(me_f * 4, 4), 4)
    kept = pltpu.make_async_copy(send_r.at[me_four], recv_r.at[me_four], local_sem.at[5])
    kept.start()
    zl = wrapped(z - 4 * z_hi, 4)
    for dx in XY_ORDER:
        for dy in XY_ORDER:
            for dz in (3, 1, 2, 0):
                if (dx, dy, dz) != (0, 0, 0):
                    other = x_slot[dx] + zl[dz] * 4 + ys[dy]
                    four = pl.ds(pl.multiple_of(other * 4, 4), 4)
                    remote(send_r.at[four], recv_r.at[me_four], 8, other * 4 + me_c).start()

    later[1].wait_recv()
    later[2].wait_recv()
    relay_own.wait_recv()
    relay_rest.wait_recv()
    kept.wait()
    wait_bytes(recv_r.at[pl.ds(0, 4 * G - 4)], recv_sem.at[8])

    causal = [unpack(recv_r[pl.ds(f, G, stride=4), :]) for f in range(4)]
    for f in range(FL):
        high, low = split(causal[f % 4][f // 4])
        stack = jnp.concatenate(
            [
                jnp.concatenate([high[:, :64], low[:, :64]], axis=1),
                jnp.concatenate([high[:, 64:], low[:, 64:]], axis=1),
            ],
            axis=0,
        )
        both = jnp.concatenate([psi_all[f, 0], psi_all[f, 1]], axis=0)
        got = dot_tt(stack, both)
        got = got[:64] + got[64:]
        out_ref[f, 0] = got[:32, :C] - got[32:, C:]
        out_ref[f, 1] = got[32:, :C] + got[:32, C:]

    wait_bytes(psi_all.at[pl.ds(0, OWN), :, pl.ds(0, 3 * PANEL), :], send_sem.at[0])
    wait_bytes(spec_all.at[:, :, pl.ds(0, 3 * PANEL), :], send_sem.at[1])
    for copy in later + [relay_own, relay_rest]:
        copy.wait_send()
    wait_bytes(send_f.at[pl.ds(0, 4 * G - 1)], send_sem.at[6])
    wait_bytes(send_r.at[pl.ds(0, 4 * G - 4)], send_sem.at[8])


def step(factor, spectrum, guess_scale, lag_cutoff):
    table = tables()
    vmem = pl.BlockSpec(memory_space=pltpu.VMEM)
    smem = pl.BlockSpec(memory_space=pltpu.SMEM)
    hbm = pl.BlockSpec(memory_space=pltpu.HBM)
    dma = pltpu.SemaphoreType.DMA
    out = pl.pallas_call(
        kernel,
        out_shape=jax.ShapeDtypeStruct((FL, 2, PANEL, C), F32),
        in_specs=[hbm, hbm, hbm, smem, hbm],
        out_specs=vmem,
        scratch_shapes=[
            pltpu.VMEM((OWN, 2, C, C), BF),
            pltpu.VMEM((FL, 2, C, C), BF),
            pltpu.VMEM((4 * G, C), jnp.int32),
            pltpu.VMEM((4 * G, C), jnp.int32),
            pltpu.VMEM((4 * G, C), jnp.int32),
            pltpu.VMEM((4 * G, C), jnp.int32),
            pltpu.VMEM(table.shape, BF),
            pltpu.SMEM((FL,), F32),
            pltpu.SemaphoreType.REGULAR((3,)),
            dma((6,)),
            dma((9,)),
            dma((9,)),
        ],
        compiler_params=pltpu.CompilerParams(collective_id=0, has_side_effects=True, vmem_limit_bytes=VMEM_LIMIT),
    )(factor, spectrum, guess_scale, lag_cutoff, jnp.asarray(table))
    return jnp.swapaxes(out, 2, 3)


def solution(mesh):
    in_specs = (P("freq", None, "chan", None), P("freq", None, "chan", None), P("freq"), P())
    out_specs = P("freq", None, None, "chan")
    return jax.shard_map(step, mesh=mesh, in_specs=in_specs, out_specs=out_specs, check_vma=False)
```

```python
import math

import jax
import jax.numpy as jnp
import numpy as np
from jax import lax
from jax.experimental import pallas as pl
from jax.experimental.pallas import tpu as pltpu
from jax.sharding import PartitionSpec as P

ITERS = 8
LOGICAL = pl.DeviceIdType.LOGICAL
BF = jnp.bfloat16
F32 = jnp.float32
C = 128
PANEL = 32
FL = 8
OWN = 2
G = 64
F = 512
LAGS = 256
FLOOR = 2.0**-16
STEPS = 32767 / (40 * math.log(2.0))
VMEM_LIMIT = 67043328 - 10500 * 1024
Z_ORDER = (4, 3, 5, 2, 6, 1, 7, 0)
XY_ORDER = (2, 1, 3, 0)


def rem(a, b):
    return lax.rem(a, jnp.int32(b))


def div(a, b):
    return lax.div(a, jnp.int32(b))


def coords():
    f = lax.axis_index("freq")
    c = lax.axis_index("chan")
    return div(f, 16), rem(f, 4), div(c, 2) * 4 + rem(div(f, 4), 4), rem(c, 2)


def split(value):
    high = value.astype(BF)
    return high, (value - high.astype(F32)).astype(BF)


def embed(value):
    re, im = value[:, :C], value[:, C:]
    return jnp.concatenate([value, jnp.concatenate([-im, re], axis=1)], axis=0)


def code(value):
    steps = jnp.minimum(jnp.log(1.0 + jnp.abs(value) * (1.0 / FLOOR)) * STEPS + 0.5, 32767.0).astype(jnp.int32)
    return jnp.where(value < 0, -steps, steps)


def decode(number):
    value = number.astype(F32)
    size = FLOOR * jnp.exp(jnp.abs(value) * (1.0 / STEPS)) - FLOOR
    return jnp.where(number < 0, -size, size)


def pack(low, high):
    return code(low) + (code(high) << 16)


def unpack(word):
    low = (word << 16) >> 16
    return decode(low), decode((word - low) >> 16)


def dot(left, right):
    return jnp.dot(left, right, preferred_element_type=F32)


def dot_nt(left, right):
    return lax.dot_general(left, right, (((1,), (1,)), ((), ())), preferred_element_type=F32)


def dot_tn(left, right):
    return lax.dot_general(left, right, (((0,), (0,)), ((), ())), preferred_element_type=F32)


def dot_tt(left, right):
    return lax.dot_general(left, right, (((0,), (1,)), ((), ())), preferred_element_type=F32)


def tables():
    to_lag, to_freq = [], []
    pairs = np.arange(C).reshape(C // 2, 2).T.reshape(-1)
    fours = np.arange(C).reshape(C // 8, 2, 4).swapaxes(0, 1).reshape(-1)
    for r in range(4):
        lag = 4 * np.arange(LAGS // 4) + r
        angle = 2.0 * np.pi * (np.outer(lag, pairs) % F) / F
        to_lag.append(np.concatenate([np.cos(angle), np.sin(angle)], axis=0) / F)
        angle = 2.0 * np.pi * (np.outer(lag, fours) % F) / F
        to_freq.append(np.concatenate([np.cos(angle).T, -np.sin(angle).T], axis=1))
    table = np.concatenate(to_lag + to_freq, axis=0)
    high = table.astype(jnp.bfloat16)
    low = (table - high.astype(np.float64)).astype(jnp.bfloat16)
    return np.concatenate([high, low], axis=0)


def turn(value):
    lane = lax.broadcasted_iota(jnp.int32, value.shape, 1)
    return jnp.where(rem(lane, 64) < 32, -pltpu.roll(value, 96, 1), pltpu.roll(value, 32, 1))


def table_dot(table_ref, block, value):
    high, low = split(value)
    first = dot(table_ref[pl.ds(C * block, C), :], jnp.concatenate([high, low], axis=1))
    return first[:, :C] + first[:, C:] + dot(table_ref[pl.ds(C * (block + 8), C), :], high)


def project(table_ref, m, cutoff):
    even, odd, even_d, odd_d = m[0] + m[2], m[1] + m[3], m[0] - m[2], turn(m[1] - m[3])
    sums = [even + odd, even_d + odd_d, even - odd, even_d - odd_d]
    row = lax.broadcasted_iota(jnp.int32, (LAGS // 4, C), 0)
    back = []
    for r in range(4):
        both = table_dot(table_ref, r, sums[r])
        lag = 4 * row + r
        keep = jnp.where(lag == 0, 0.5, jnp.where(lag <= cutoff, 1.0, 0.0)).astype(F32)
        lags = (both[: LAGS // 4] + turn(both[LAGS // 4 :])) * keep
        back.append(table_dot(table_ref, 4 + r, jnp.concatenate([lags, turn(lags)], axis=0)))
    even, odd, even_d, odd_d = back[0] + back[2], back[1] + back[3], back[0] - back[2], turn(back[1] - back[3])
    return [even + odd, even_d - odd_d, even - odd, even_d + odd_d]


def kernel(
    factor_ref, spectrum_ref, scale_hbm, cutoff_ref, table_hbm, out_0, out_1, out_2, out_3,
    spec_all, psi_all, send_f, recv_f, send_r, recv_r, table, scale_ref, stage_sem, local_sem, send_sem, recv_sem,
):
    x, y, z, k = coords()
    me_f = lax.axis_index("freq")
    me_c = lax.axis_index("chan")
    me_lin = me_f * 4 + me_c
    z_hi = div(me_c, 2)

    def wrapped(value, size):
        return [value] + [value + i - jnp.where(value >= size - i, size, 0) for i in range(1, size)]

    xs, ys, zs = wrapped(x, 4), wrapped(y, 4), wrapped(z, 8)
    zh = [jnp.where(v >= 4, 1, 0) for v in zs]
    x_part = [v * 64 for v in xs]
    y_part = [v * 4 for v in ys]
    z_part = [v * 16 - h * 62 for v, h in zip(zs, zh)]
    k_part = [k, 1 - k]

    def number(dx, dy, dz, dk):
        return x_part[dx] + y_part[dy] + z_part[dz] + k_part[dk]

    on_y = [number(0, i, 0, 0) for i in (2, 1, 3)]
    on_z = [number(0, 0, i, 0) for i in Z_ORDER[:-1]]
    on_x = [number(i, 0, 0, 0) for i in (2, 1, 3)]
    sibling, across, diagonal = number(0, 0, 0, 1), number(0, 0, 4, 0), number(0, 0, 4, 1)
    sibling_c = 2 * z_hi + 1 - k
    across_c = 2 - 2 * z_hi + k
    diagonal_c = 3 - 2 * z_hi - k

    def signal(sem, peers):
        for peer in peers:
            pl.semaphore_signal(sem, inc=1, device_id=peer, device_id_type=LOGICAL)

    def remote(src, dst, i, peer):
        return pltpu.make_async_remote_copy(
            src_ref=src, dst_ref=dst, send_sem=send_sem.at[i], recv_sem=recv_sem.at[i], device_id=peer, device_id_type=LOGICAL
        )

    def wait_bytes(ref, sem):
        pltpu.make_async_copy(ref, ref, sem).wait()

    barrier = pltpu.get_barrier_semaphore()
    first_peers = [diagonal] + on_z + on_x + on_y + [sibling]
    signal(barrier, first_peers)

    def panel_rows(chan):
        return pl.ds(pl.multiple_of(chan * PANEL, PANEL), PANEL)

    def own_freqs(chan):
        return pl.ds(OWN * chan, OWN)

    my_rows = panel_rows(me_c)
    own_copies = [
        pltpu.make_async_copy(factor_ref, psi_all.at[:, :, my_rows, :], local_sem.at[0]),
        pltpu.make_async_copy(spectrum_ref.at[own_freqs(me_c)], spec_all.at[:, :, my_rows, :], local_sem.at[1]),
    ]
    scale_in = pltpu.make_async_copy(scale_hbm, scale_ref, local_sem.at[2])
    table_in = pltpu.make_async_copy(table_hbm, table, local_sem.at[3])
    for copy in own_copies + [scale_in, table_in]:
        copy.start()

    pl.semaphore_wait(barrier, len(first_peers))
    partners = ((across, across_c), (diagonal, diagonal_c), (sibling, sibling_c))
    for peer, chan in partners:
        freqs = own_freqs(chan)
        remote(factor_ref.at[freqs], psi_all.at[freqs, :, my_rows, :], 0, peer).start()
    for peer, chan in partners:
        remote(spectrum_ref.at[own_freqs(chan)], spec_all.at[:, :, my_rows, :], 1, peer).start()
    mine = own_freqs(me_c)
    here_half = pl.ds(4 * z_hi, 4)
    there_half = pl.ds(4 - 4 * z_hi, 4)
    later = [
        remote(factor_ref.at[here_half], psi_all.at[here_half, :, my_rows, :], 2, across),
        remote(factor_ref.at[there_half], psi_all.at[there_half, :, my_rows, :], 3, sibling),
        remote(factor_ref.at[mine], psi_all.at[mine, :, my_rows, :], 4, sibling),
    ]
    for copy in later:
        copy.start()

    signal(stage_sem.at[0], [sibling])
    pl.semaphore_wait(stage_sem.at[0], 1)
    signal(stage_sem.at[1], on_y)
    pl.semaphore_wait(stage_sem.at[1], 3)
    signal(stage_sem.at[2], on_z)

    own_copies[0].wait()
    scale_in.wait()
    wait_bytes(psi_all.at[pl.ds(0, OWN), :, pl.ds(0, 3 * PANEL), :], recv_sem.at[0])
    there_rows = pl.ds(pl.multiple_of(64 - 64 * z_hi, 64), 64)
    got = psi_all.at[mine, :, there_rows, :]
    relay_own = remote(got, got, 5, sibling)
    relay_own.start()

    row = lax.broadcasted_iota(jnp.int32, (C, 2 * C), 0)
    col = lax.broadcasted_iota(jnp.int32, (C, 2 * C), 1)
    eye = (row == col).astype(F32)
    lane = lax.broadcasted_iota(jnp.int32, (G, C), 1)

    psis, rs, qs = [], [], []
    for b in range(OWN):
        psi = jnp.concatenate([psi_all[OWN * me_c + b, 0], psi_all[OWN * me_c + b, 1]], axis=1)
        wide = embed(psi)
        r = eye - scale_ref[OWN * me_c + b] * dot_nt(psi, wide)
        psis.append(wide)
        rs.append(r)
        qs.append(eye + r)

    def times(left, right_high, right_low):
        high, low = split(left)
        e_high, e_low = embed(right_high), embed(right_low)
        rows = left.shape[0]
        most = dot(jnp.concatenate([high, low], axis=0), e_high)
        return most[:rows] + (most[rows:] + dot(high, e_low))

    for step in range(ITERS):
        for b in range(OWN):
            right = split(rs[b])
            if step == 0:
                rs[b] = times(rs[b], *right)
            elif step < ITERS - 1:
                both = times(jnp.concatenate([rs[b], qs[b]], axis=0), *right)
                rs[b] = both[:C]
                qs[b] = qs[b] + both[C:]
            else:
                qs[b] = qs[b] + times(qs[b], *right)

    def upright(value):
        return jnp.concatenate([value[:, :C], -value[:, C:]], axis=0)

    zs_split, us_split = [], []
    for b in range(OWN):
        q_high, q_low = split(qs[b])
        zz = dot(jnp.concatenate([q_high, q_low], axis=0), psis[b])
        zs_split.append(split(scale_ref[OWN * me_c + b] * (zz[:C] + zz[C:])))
    own_copies[1].wait()
    wait_bytes(spec_all.at[:, :, pl.ds(0, 3 * PANEL), :], recv_sem.at[1])
    for b in range(OWN):
        z_high, z_low = zs_split[b]
        spec = jnp.concatenate([spec_all[b, 0], spec_all[b, 1]], axis=1)
        u = dot(
            jnp.concatenate([spec, spec], axis=1), jnp.concatenate([embed(z_high), embed(z_low)], axis=0)
        )
        us_split.append(split(u))
    mids = []
    for b in range(OWN):
        zs_high, zs_low = upright(zs_split[b][0]), upright(zs_split[b][1])
        eu_high, eu_low = embed(us_split[b][0]), embed(us_split[b][1])
        mids.append(
            eye
            + dot_tn(
                jnp.concatenate([zs_high, zs_low, zs_high], axis=0), jnp.concatenate([eu_high, eu_high, eu_low], axis=0)
            )
        )
    half = C // 2
    words = [pack(mids[0][:, :C], mids[1][:, :C]), pack(mids[0][:, C:], mids[1][:, C:])]
    pieces = [words[0][:half], words[1][:half], words[0][half:], words[1][half:]]
    for j in range(4):
        rolled = []
        for i, piece in enumerate(pieces):
            shift = (32 * i - 32 * j) % C
            rolled.append(pltpu.roll(piece, shift, 1) if shift else piece)
        send_f[pl.ds(G * j, G), :] = jnp.where(
            lane < 64,
            jnp.where(lane < 32, rolled[0], rolled[1]),
            jnp.where(lane < 96, rolled[2], rolled[3]),
        )

    x_slot = [v * 16 for v in xs]
    z_slot = [v * 4 + h * 112 for v, h in zip(zs, zh)]
    k_slot = [k * 64, 64 - k * 64]
    pl.semaphore_wait(stage_sem.at[2], len(on_z))
    kept = pltpu.make_async_copy(send_f.at[pl.ds(me_c * G + me_f, 1)], recv_f.at[pl.ds(me_lin, 1)], local_sem.at[4])
    kept.start()
    for dx in XY_ORDER:
        for dy in XY_ORDER:
            for dk in (1, 0):
                for dz in Z_ORDER:
                    if (dx, dy, dz, dk) != (0, 0, 0, 0):
                        slot = x_slot[dx] + ys[dy] + z_slot[dz] + k_slot[dk]
                        remote(send_f.at[pl.ds(slot, 1)], recv_f.at[pl.ds(me_lin, 1)], 6, number(dx, dy, dz, dk)).start()

    got = psi_all.at[there_half, :, panel_rows(across_c), :]
    wait_bytes(got, recv_sem.at[2])
    relay_rest = remote(got, got, 7, sibling)
    relay_rest.start()

    table_in.wait()
    kept.wait()
    wait_bytes(recv_f.at[pl.ds(0, 4 * G - 1)], recv_sem.at[6])

    even, odd = unpack(recv_f[...])
    blocks = [jnp.concatenate([even[G * i : G * (i + 1)], odd[G * i : G * (i + 1)]], axis=0) for i in range(4)]
    parts = project(table, blocks, cutoff_ref[0])
    for i in range(4):
        send_r[pl.ds(G * i, G), :] = pack(parts[i][:G], parts[i][G:])

    me_four = pl.ds(pl.multiple_of(me_f * 4, 4), 4)
    kept = pltpu.make_async_copy(send_r.at[me_four], recv_r.at[me_four], local_sem.at[5])
    kept.start()
    zl = wrapped(z - 4 * z_hi, 4)
    for dx in XY_ORDER:
        for dy in XY_ORDER:
            for dz in (3, 1, 2, 0):
                if (dx, dy, dz) != (0, 0, 0):
                    other = x_slot[dx] + zl[dz] * 4 + ys[dy]
                    four = pl.ds(pl.multiple_of(other * 4, 4), 4)
                    remote(send_r.at[four], recv_r.at[me_four], 8, other * 4 + me_c).start()

    later[1].wait_recv()
    later[2].wait_recv()
    relay_own.wait_recv()
    relay_rest.wait_recv()
    kept.wait()
    wait_bytes(recv_r.at[pl.ds(0, 4 * G - 4)], recv_sem.at[8])

    causal = [unpack(recv_r[pl.ds(f, G, stride=4), :]) for f in range(4)]
    outs = (out_0, out_1, out_2, out_3)
    for f in range(FL):
        out_ref = outs[f // 2]
        high, low = split(causal[f % 4][f // 4])
        stack = jnp.concatenate(
            [
                jnp.concatenate([high[:, :64], low[:, :64]], axis=1),
                jnp.concatenate([high[:, 64:], low[:, 64:]], axis=1),
            ],
            axis=0,
        )
        both = jnp.concatenate([psi_all[f, 0], psi_all[f, 1]], axis=0)
        got = dot_tt(stack, both)
        got = got[:64] + got[64:]
        out_ref[f % 2, 0] = got[:32, :C] - got[32:, C:]
        out_ref[f % 2, 1] = got[32:, :C] + got[:32, C:]

    wait_bytes(psi_all.at[pl.ds(0, OWN), :, pl.ds(0, 3 * PANEL), :], send_sem.at[0])
    wait_bytes(spec_all.at[:, :, pl.ds(0, 3 * PANEL), :], send_sem.at[1])
    for copy in later + [relay_own, relay_rest]:
        copy.wait_send()
    wait_bytes(send_f.at[pl.ds(0, 4 * G - 1)], send_sem.at[6])
    wait_bytes(send_r.at[pl.ds(0, 4 * G - 4)], send_sem.at[8])


def step(factor, spectrum, guess_scale, lag_cutoff):
    table = tables()
    vmem = pl.BlockSpec(memory_space=pltpu.VMEM)
    smem = pl.BlockSpec(memory_space=pltpu.SMEM)
    hbm = pl.BlockSpec(memory_space=pltpu.HBM)
    dma = pltpu.SemaphoreType.DMA
    outs = pl.pallas_call(
        kernel,
        out_shape=[jax.ShapeDtypeStruct((2, 2, PANEL, C), F32)] * 4,
        in_specs=[hbm, hbm, hbm, smem, hbm],
        out_specs=[vmem] * 4,
        scratch_shapes=[
            pltpu.VMEM((OWN, 2, C, C), BF),
            pltpu.VMEM((FL, 2, C, C), BF),
            pltpu.VMEM((4 * G, C), jnp.int32),
            pltpu.VMEM((4 * G, C), jnp.int32),
            pltpu.VMEM((4 * G, C), jnp.int32),
            pltpu.VMEM((4 * G, C), jnp.int32),
            pltpu.VMEM(table.shape, BF),
            pltpu.SMEM((FL,), F32),
            pltpu.SemaphoreType.REGULAR((3,)),
            dma((6,)),
            dma((9,)),
            dma((9,)),
        ],
        compiler_params=pltpu.CompilerParams(collective_id=0, has_side_effects=True, vmem_limit_bytes=VMEM_LIMIT),
    )(factor, spectrum, guess_scale, lag_cutoff, jnp.asarray(table))
    return jnp.swapaxes(jnp.concatenate(outs, axis=0), 2, 3)


def solution(mesh):
    in_specs = (P("freq", None, "chan", None), P("freq", None, "chan", None), P("freq"), P())
    out_specs = P("freq", None, None, "chan")
    return jax.shard_map(step, mesh=mesh, in_specs=in_specs, out_specs=out_specs, check_vma=False)
```

```python
import jax
import jax.numpy as jnp
import numpy as np
from jax import lax
from jax.experimental import pallas as pl
from jax.experimental.pallas import tpu as pltpu
from jax.sharding import PartitionSpec as P

ITERS = 8
LOGICAL = pl.DeviceIdType.LOGICAL
BF = jnp.bfloat16
F32 = jnp.float32
C = 128
PANEL = 32
FL = 8
OWN = 2
G = 64
F = 512
LAGS = 256
FLOOR = 2.0**-16
STEPS = 32767 / 40
VMEM_LIMIT = 67043328 - 10500 * 1024
Z_ORDER = (4, 3, 5, 2, 6, 1, 7, 0)
XY_ORDER = (2, 1, 3, 0)


def rem(a, b):
    return lax.rem(a, jnp.int32(b))


def div(a, b):
    return lax.div(a, jnp.int32(b))


def coords():
    f = lax.axis_index("freq")
    c = lax.axis_index("chan")
    return div(f, 16), rem(f, 4), div(c, 2) * 4 + rem(div(f, 4), 4), rem(c, 2)


def split(value):
    high = value.astype(BF)
    return high, (value - high.astype(F32)).astype(BF)


def embed(value):
    re, im = value[:, :C], value[:, C:]
    return jnp.concatenate([value, jnp.concatenate([-im, re], axis=1)], axis=0)


def code(value):
    steps = jnp.minimum(jnp.log2(1.0 + jnp.abs(value) * (1.0 / FLOOR)) * STEPS + 0.5, 32767.0).astype(jnp.int32)
    return jnp.where(value < 0, -steps, steps)


def decode(number):
    value = number.astype(F32)
    size = jnp.exp2(jnp.abs(value) * (1.0 / STEPS) - 16.0) - FLOOR
    return jnp.where(number < 0, -size, size)


def pack(low, high):
    return code(low) + (code(high) << 16)


def unpack(word):
    low = (word << 16) >> 16
    return decode(low), decode((word - low) >> 16)


def dot(left, right):
    return jnp.dot(left, right, preferred_element_type=F32)


def dot_nt(left, right):
    return lax.dot_general(left, right, (((1,), (1,)), ((), ())), preferred_element_type=F32)


def dot_tn(left, right):
    return lax.dot_general(left, right, (((0,), (0,)), ((), ())), preferred_element_type=F32)


def dot_tt(left, right):
    return lax.dot_general(left, right, (((0,), (1,)), ((), ())), preferred_element_type=F32)


def tables():
    to_lag, to_freq = [], []
    pairs = np.arange(C).reshape(C // 2, 2).T.reshape(-1)
    fours = np.arange(C).reshape(C // 8, 2, 4).swapaxes(0, 1).reshape(-1)
    for r in range(4):
        lag = 4 * np.arange(LAGS // 4) + r
        angle = 2.0 * np.pi * (np.outer(lag, pairs) % F) / F
        to_lag.append(np.concatenate([np.cos(angle), np.sin(angle)], axis=0) / F)
        angle = 2.0 * np.pi * (np.outer(lag, fours) % F) / F
        to_freq.append(np.concatenate([np.cos(angle).T, -np.sin(angle).T], axis=1))
    table = np.concatenate(to_lag + to_freq, axis=0)
    high = table.astype(jnp.bfloat16)
    low = (table - high.astype(np.float64)).astype(jnp.bfloat16)
    return np.concatenate([high, low], axis=0)


def turn(value):
    lane = lax.broadcasted_iota(jnp.int32, value.shape, 1)
    return jnp.where(rem(lane, 64) < 32, -pltpu.roll(value, 96, 1), pltpu.roll(value, 32, 1))


def table_dot(table_ref, block, value):
    high, low = split(value)
    first = dot(table_ref[pl.ds(C * block, C), :], jnp.concatenate([high, low], axis=1))
    return first[:, :C] + first[:, C:] + dot(table_ref[pl.ds(C * (block + 8), C), :], high)


def project(table_ref, m, cutoff):
    even, odd, even_d, odd_d = m[0] + m[2], m[1] + m[3], m[0] - m[2], turn(m[1] - m[3])
    sums = [even + odd, even_d + odd_d, even - odd, even_d - odd_d]
    row = lax.broadcasted_iota(jnp.int32, (LAGS // 4, C), 0)
    back = []
    for r in range(4):
        both = table_dot(table_ref, r, sums[r])
        lag = 4 * row + r
        keep = jnp.where(lag == 0, 0.5, jnp.where(lag <= cutoff, 1.0, 0.0)).astype(F32)
        lags = (both[: LAGS // 4] + turn(both[LAGS // 4 :])) * keep
        back.append(table_dot(table_ref, 4 + r, jnp.concatenate([lags, turn(lags)], axis=0)))
    even, odd, even_d, odd_d = back[0] + back[2], back[1] + back[3], back[0] - back[2], turn(back[1] - back[3])
    return [even + odd, even_d - odd_d, even - odd, even_d + odd_d]


def kernel(
    factor_ref, spectrum_ref, scale_hbm, cutoff_ref, table_hbm, out_0, out_1, out_2, out_3,
    spec_all, psi_all, send_f, recv_f, part_all, send_r, recv_r, table, scale_ref, stage_sem, local_sem, send_sem, recv_sem,
):
    x, y, z, k = coords()
    me_f = lax.axis_index("freq")
    me_c = lax.axis_index("chan")
    me_lin = me_f * 4 + me_c
    z_hi = div(me_c, 2)

    def wrapped(value, size):
        return [value] + [value + i - jnp.where(value >= size - i, size, 0) for i in range(1, size)]

    xs, ys, zs = wrapped(x, 4), wrapped(y, 4), wrapped(z, 8)
    zh = [jnp.where(v >= 4, 1, 0) for v in zs]
    x_part = [v * 64 for v in xs]
    y_part = [v * 4 for v in ys]
    z_part = [v * 16 - h * 62 for v, h in zip(zs, zh)]
    k_part = [k, 1 - k]

    def number(dx, dy, dz, dk):
        return x_part[dx] + y_part[dy] + z_part[dz] + k_part[dk]

    on_y = [number(0, i, 0, 0) for i in (2, 1, 3)]
    on_z = [number(0, 0, i, 0) for i in Z_ORDER[:-1]]
    on_x = [number(i, 0, 0, 0) for i in (2, 1, 3)]
    sibling, across, diagonal = number(0, 0, 0, 1), number(0, 0, 4, 0), number(0, 0, 4, 1)
    sibling_c = 2 * z_hi + 1 - k
    across_c = 2 - 2 * z_hi + k
    diagonal_c = 3 - 2 * z_hi - k

    def signal(sem, peers):
        for peer in peers:
            pl.semaphore_signal(sem, inc=1, device_id=peer, device_id_type=LOGICAL)

    def remote(src, dst, i, peer):
        return pltpu.make_async_remote_copy(
            src_ref=src, dst_ref=dst, send_sem=send_sem.at[i], recv_sem=recv_sem.at[i], device_id=peer, device_id_type=LOGICAL
        )

    def wait_bytes(ref, sem):
        pltpu.make_async_copy(ref, ref, sem).wait()

    barrier = pltpu.get_barrier_semaphore()
    first_peers = [diagonal] + on_z + on_x + on_y + [sibling]
    signal(barrier, first_peers)

    def panel_rows(chan):
        return pl.ds(pl.multiple_of(chan * PANEL, PANEL), PANEL)

    def own_freqs(chan):
        return pl.ds(OWN * chan, OWN)

    my_rows = panel_rows(me_c)
    own_copies = [
        pltpu.make_async_copy(factor_ref, psi_all.at[:, :, my_rows, :], local_sem.at[0]),
        pltpu.make_async_copy(spectrum_ref.at[own_freqs(me_c)], spec_all.at[:, :, my_rows, :], local_sem.at[1]),
    ]
    scale_in = pltpu.make_async_copy(scale_hbm, scale_ref, local_sem.at[2])
    table_in = pltpu.make_async_copy(table_hbm, table, local_sem.at[3])
    for copy in own_copies + [scale_in, table_in]:
        copy.start()

    pl.semaphore_wait(barrier, len(first_peers))
    partners = ((across, across_c), (diagonal, diagonal_c), (sibling, sibling_c))
    for peer, chan in partners:
        freqs = own_freqs(chan)
        remote(factor_ref.at[freqs], psi_all.at[freqs, :, my_rows, :], 0, peer).start()
    for peer, chan in partners:
        remote(spectrum_ref.at[own_freqs(chan)], spec_all.at[:, :, my_rows, :], 1, peer).start()
    mine = own_freqs(me_c)
    here_half = pl.ds(4 * z_hi, 4)
    there_half = pl.ds(4 - 4 * z_hi, 4)
    later = [
        remote(factor_ref.at[here_half], psi_all.at[here_half, :, my_rows, :], 2, across),
        remote(factor_ref.at[there_half], psi_all.at[there_half, :, my_rows, :], 3, sibling),
        remote(factor_ref.at[mine], psi_all.at[mine, :, my_rows, :], 4, sibling),
    ]
    for copy in later:
        copy.start()

    signal(stage_sem.at[0], [sibling])
    pl.semaphore_wait(stage_sem.at[0], 1)
    signal(stage_sem.at[1], on_y)
    pl.semaphore_wait(stage_sem.at[1], 3)
    signal(stage_sem.at[2], on_z)

    own_copies[0].wait()
    scale_in.wait()
    wait_bytes(psi_all.at[pl.ds(0, OWN), :, pl.ds(0, 3 * PANEL), :], recv_sem.at[0])
    there_rows = pl.ds(pl.multiple_of(64 - 64 * z_hi, 64), 64)
    got = psi_all.at[mine, :, there_rows, :]
    relay_own = remote(got, got, 5, sibling)
    relay_own.start()

    row = lax.broadcasted_iota(jnp.int32, (C, 2 * C), 0)
    col = lax.broadcasted_iota(jnp.int32, (C, 2 * C), 1)
    eye = (row == col).astype(F32)
    lane = lax.broadcasted_iota(jnp.int32, (G, C), 1)

    psis, rs, qs = [], [], []
    for b in range(OWN):
        psi = jnp.concatenate([psi_all[OWN * me_c + b, 0], psi_all[OWN * me_c + b, 1]], axis=1)
        wide = embed(psi)
        r = eye - scale_ref[OWN * me_c + b] * dot_nt(psi, wide)
        psis.append(wide)
        rs.append(r)
        qs.append(eye + r)

    def times(left, right_high, right_low):
        high, low = split(left)
        e_high, e_low = embed(right_high), embed(right_low)
        rows = left.shape[0]
        most = dot(jnp.concatenate([high, low], axis=0), e_high)
        return most[:rows] + (most[rows:] + dot(high, e_low))

    for step in range(ITERS):
        for b in range(OWN):
            right = split(rs[b])
            if step == 0:
                rs[b] = times(rs[b], *right)
            elif step < ITERS - 1:
                both = times(jnp.concatenate([rs[b], qs[b]], axis=0), *right)
                rs[b] = both[:C]
                qs[b] = qs[b] + both[C:]
            else:
                qs[b] = qs[b] + times(qs[b], *right)

    def upright(value):
        return jnp.concatenate([value[:, :C], -value[:, C:]], axis=0)

    zs_split, us_split = [], []
    for b in range(OWN):
        q_high, q_low = split(qs[b])
        zz = dot(jnp.concatenate([q_high, q_low], axis=0), psis[b])
        zs_split.append(split(scale_ref[OWN * me_c + b] * (zz[:C] + zz[C:])))
    own_copies[1].wait()
    wait_bytes(spec_all.at[:, :, pl.ds(0, 3 * PANEL), :], recv_sem.at[1])
    for b in range(OWN):
        z_high, z_low = zs_split[b]
        spec = jnp.concatenate([spec_all[b, 0], spec_all[b, 1]], axis=1)
        u = dot(
            jnp.concatenate([spec, spec], axis=1), jnp.concatenate([embed(z_high), embed(z_low)], axis=0)
        )
        us_split.append(split(u))
    mids = []
    for b in range(OWN):
        zs_high, zs_low = upright(zs_split[b][0]), upright(zs_split[b][1])
        eu_high, eu_low = embed(us_split[b][0]), embed(us_split[b][1])
        mids.append(
            eye
            + dot_tn(
                jnp.concatenate([zs_high, zs_low, zs_high], axis=0), jnp.concatenate([eu_high, eu_high, eu_low], axis=0)
            )
        )
    half = C // 2
    words = [pack(mids[0][:, :C], mids[1][:, :C]), pack(mids[0][:, C:], mids[1][:, C:])]
    pieces = [words[0][:half], words[1][:half], words[0][half:], words[1][half:]]
    for j in range(4):
        rolled = []
        for i, piece in enumerate(pieces):
            shift = (32 * i - 32 * j) % C
            rolled.append(pltpu.roll(piece, shift, 1) if shift else piece)
        send_f[pl.ds(G * j, G), :] = jnp.where(
            lane < 64,
            jnp.where(lane < 32, rolled[0], rolled[1]),
            jnp.where(lane < 96, rolled[2], rolled[3]),
        )

    x_slot = [v * 16 for v in xs]
    z_slot = [v * 4 + h * 112 for v, h in zip(zs, zh)]
    k_slot = [k * 64, 64 - k * 64]
    pl.semaphore_wait(stage_sem.at[2], len(on_z))
    kept = pltpu.make_async_copy(send_f.at[pl.ds(me_c * G + me_f, 1)], recv_f.at[pl.ds(me_lin, 1)], local_sem.at[4])
    kept.start()
    for dx in XY_ORDER:
        for dy in XY_ORDER:
            for dk in (1, 0):
                for dz in Z_ORDER:
                    if (dx, dy, dz, dk) != (0, 0, 0, 0):
                        slot = x_slot[dx] + ys[dy] + z_slot[dz] + k_slot[dk]
                        remote(send_f.at[pl.ds(slot, 1)], recv_f.at[pl.ds(me_lin, 1)], 6, number(dx, dy, dz, dk)).start()

    got = psi_all.at[there_half, :, panel_rows(across_c), :]
    wait_bytes(got, recv_sem.at[2])
    relay_rest = remote(got, got, 7, sibling)
    relay_rest.start()

    table_in.wait()
    kept.wait()
    wait_bytes(recv_f.at[pl.ds(0, 4 * G - 1)], recv_sem.at[6])

    even, odd = unpack(recv_f[...])
    blocks = [jnp.concatenate([even[G * i : G * (i + 1)], odd[G * i : G * (i + 1)]], axis=0) for i in range(4)]
    parts = project(table, blocks, cutoff_ref[0])
    for i in range(4):
        part_all[i] = parts[i]

    me_four = pl.ds(pl.multiple_of(me_f * 4, 4), 4)
    zl = wrapped(z - 4 * z_hi, 4)
    for dx in XY_ORDER:
        part = part_all[xs[dx]]
        send_r[pl.ds(pl.multiple_of(xs[dx] * G, G), G), :] = pack(part[:G], part[G:])
        for dy in XY_ORDER:
            for dz in (3, 1, 2, 0):
                if (dx, dy, dz) != (0, 0, 0):
                    other = x_slot[dx] + zl[dz] * 4 + ys[dy]
                    four = pl.ds(pl.multiple_of(other * 4, 4), 4)
                    remote(send_r.at[four], recv_r.at[me_four], 8, other * 4 + me_c).start()

    kept = pltpu.make_async_copy(send_r.at[me_four], recv_r.at[me_four], local_sem.at[5])
    kept.start()
    later[1].wait_recv()
    later[2].wait_recv()
    relay_own.wait_recv()
    relay_rest.wait_recv()
    kept.wait()
    wait_bytes(recv_r.at[pl.ds(0, 4 * G - 4)], recv_sem.at[8])

    causal = [unpack(recv_r[pl.ds(f, G, stride=4), :]) for f in range(4)]
    outs = (out_0, out_1, out_2, out_3)
    for f in range(FL):
        out_ref = outs[f // 2]
        high, low = split(causal[f % 4][f // 4])
        stack = jnp.concatenate(
            [
                jnp.concatenate([high[:, :64], low[:, :64]], axis=1),
                jnp.concatenate([high[:, 64:], low[:, 64:]], axis=1),
            ],
            axis=0,
        )
        both = jnp.concatenate([psi_all[f, 0], psi_all[f, 1]], axis=0)
        got = dot_tt(stack, both)
        got = got[:64] + got[64:]
        out_ref[f % 2, 0] = got[:32, :C] - got[32:, C:]
        out_ref[f % 2, 1] = got[32:, :C] + got[:32, C:]

    wait_bytes(psi_all.at[pl.ds(0, OWN), :, pl.ds(0, 3 * PANEL), :], send_sem.at[0])
    wait_bytes(spec_all.at[:, :, pl.ds(0, 3 * PANEL), :], send_sem.at[1])
    for copy in later + [relay_own, relay_rest]:
        copy.wait_send()
    wait_bytes(send_f.at[pl.ds(0, 4 * G - 1)], send_sem.at[6])
    wait_bytes(send_r.at[pl.ds(0, 4 * G - 4)], send_sem.at[8])


def step(factor, spectrum, guess_scale, lag_cutoff):
    table = tables()
    vmem = pl.BlockSpec(memory_space=pltpu.VMEM)
    smem = pl.BlockSpec(memory_space=pltpu.SMEM)
    hbm = pl.BlockSpec(memory_space=pltpu.HBM)
    dma = pltpu.SemaphoreType.DMA
    outs = pl.pallas_call(
        kernel,
        out_shape=[jax.ShapeDtypeStruct((2, 2, PANEL, C), F32)] * 4,
        in_specs=[hbm, hbm, hbm, smem, hbm],
        out_specs=[vmem] * 4,
        scratch_shapes=[
            pltpu.VMEM((OWN, 2, C, C), BF),
            pltpu.VMEM((FL, 2, C, C), BF),
            pltpu.VMEM((4 * G, C), jnp.int32),
            pltpu.VMEM((4 * G, C), jnp.int32),
            pltpu.VMEM((4, C, C), F32),
            pltpu.VMEM((4 * G, C), jnp.int32),
            pltpu.VMEM((4 * G, C), jnp.int32),
            pltpu.VMEM(table.shape, BF),
            pltpu.SMEM((FL,), F32),
            pltpu.SemaphoreType.REGULAR((3,)),
            dma((6,)),
            dma((9,)),
            dma((9,)),
        ],
        compiler_params=pltpu.CompilerParams(collective_id=0, has_side_effects=True, vmem_limit_bytes=VMEM_LIMIT),
    )(factor, spectrum, guess_scale, lag_cutoff, jnp.asarray(table))
    return jnp.swapaxes(jnp.concatenate(outs, axis=0), 2, 3)


def solution(mesh):
    in_specs = (P("freq", None, "chan", None), P("freq", None, "chan", None), P("freq"), P())
    out_specs = P("freq", None, None, "chan")
    return jax.shard_map(step, mesh=mesh, in_specs=in_specs, out_specs=out_specs, check_vma=False)
```
